32 devices in a mesh: gx: 4 (over y, x), gy: 8 (over z, core).
Axes of the slice: x: 2, y: 2, z: 4, core: 2. Of those that a mesh axis runs over, the one named last changes fastest.
Arguments:
- operator_t: bfloat16 [64, 512, 2432], P('gx', 'gy'), may hold values from -0.046875 to 0.046875
- data_columns: bfloat16 [2432, 384], P(('gx', 'gy')), may hold values from -6 to 6
- noise_var: float32 [2432], P(('gx', 'gy')), may hold values from 0.05 to 0.5
- class_map: int32 [64, 512], P('gx', 'gy'), may hold values from 0 to 15
- diffusion_table: float32 [16], replicated, may hold values from 0.5 to 4
- kappa_table: float32 [16], replicated, may hold values from 0.02 to 0.3
Outputs:
- hessian_block: float32 [2432, 384], P(('gx', 'gy'))
- prior_field: float32 [64, 512, 384], P('gx', 'gy')
The draws below stay inside these ranges and needn't reach their ends.
All inputs are finite; a program needn't handle non-finite values.
Results may differ from the reference program's by a relative error of at most 0.0003.
Values may be sent and summed in bfloat16 or wider, within the bound.
A program may use at most 64 MiB of HBM per device.

```python
import math
import jax
import jax.numpy as jnp
from jax import lax

K = 384
ITERS = 8
CLASSES = 16
NDATA = 2432
NX = 64
NY = 512


def place_ends(values, key, low, largest):
    place = [jax.random.randint(jax.random.fold_in(key, axis), (), 0, length) for axis, length in enumerate(values.shape)]
    main_axis = values.shape.index(max(values.shape))
    neighbour = place[:main_axis] + [(place[main_axis] + 1) % values.shape[main_axis]] + place[main_axis + 1:]
    return values.at[tuple(place)].set(low).at[tuple(neighbour)].set(largest)


def spiked(drawn, key, source, target, parts, factor):
    owner, partner = [(jnp.arange(drawn.shape[position]) // (drawn.shape[position] // parts)).reshape([-1 if axis == position else 1 for axis in range(drawn.ndim)]) for position in (source, target)]
    chosen = jax.random.permutation(key, parts)[partner]
    strong = (owner == chosen) | (owner == (partner + parts // 2) % parts)
    return jnp.where(strong, factor * drawn, drawn)


def level_of(key, shape, shards, least, largest):
    def one(axis_at, shards_of):
        steps = jax.random.uniform(jax.random.fold_in(jax.random.fold_in(key, 6), axis_at), (shards_of,), jnp.float32, least / len(shards), largest / len(shards))
        return jnp.repeat(jnp.exp(steps), shape[axis_at] // shards_of).reshape((-1,) + (1,) * (len(shape) - axis_at - 1))

    gain = one(*shards[0])
    for cut in shards[1:]:
        gain = gain * one(*cut)
    return gain


def centred(key, shape, scale, limit, cuts=(), kind=jnp.bfloat16):
    factor_of = level_of(key, shape, cuts, -0.22, 0.18) if cuts else 1.0
    result = jax.random.normal(key, shape, jnp.float32) * scale * factor_of
    return jnp.minimum(jnp.maximum(result, -limit), limit).astype(kind)


def heavy_noise(key, extent, spread, limit, pieces, heavy, kind=jnp.bfloat16):
    values = spread * jax.random.normal(key, extent, jnp.float32)
    if pieces:
        values = values * level_of(key, extent, pieces, -0.22, 0.18)
    return jnp.clip(spiked(values, jax.random.fold_in(key, 3), *heavy), -limit, limit).astype(kind)


def setup_inputs(seed: int = 0) -> dict:
    streams_of = jax.random.split(jax.random.key(seed), 7)
    operator_t = heavy_noise(streams_of[0], (NX, NY, NDATA), (NX * NY) ** -0.5, 0.046875, ((0, 4), (1, 8)), (1, 2, 8, 2.0))
    data_columns = centred(streams_of[1], (NDATA, K), 1.0, 6.0, ((0, 32),))
    noise_var = jnp.clip(jnp.exp(math.log(0.5) - 2.3025851 * jax.random.uniform(streams_of[2], (NDATA,), jnp.float32) ** level_of(streams_of[2], (NDATA,), ((0, 32),), -0.2, 0.2)), 0.05, 0.5)
    class_map = place_ends(jax.random.randint(streams_of[3], (NX, NY), 0, CLASSES), jax.random.fold_in(streams_of[3], 1), 0, CLASSES - 1).astype(jnp.int32)
    diffusion_table = jnp.clip(jnp.exp(jax.random.uniform(streams_of[4], (CLASSES,), jnp.float32, math.log(0.5), math.log(4.0))), 0.5, 4.0)
    kappa_table = jnp.clip(jnp.exp(jax.random.uniform(streams_of[5], (CLASSES,), jnp.float32, math.log(0.02), math.log(0.3))), 0.02, 0.3)
    return {"operator_t": operator_t, "data_columns": data_columns, "noise_var": noise_var, "class_map": class_map, "diffusion_table": diffusion_table, "kappa_table": kappa_table}


def lookup(classes, entries):
    onehot = (classes[..., None] == jnp.arange(entries.shape[0], dtype=jnp.int32)).astype(jnp.float32)
    return jnp.sum(onehot * entries, axis=-1)


def edge_weights(padded):
    centre = padded[1:-1, 1:-1]
    north_w = 0.5 * (centre + padded[:-2, 1:-1])
    south_w = 0.5 * (centre + padded[2:, 1:-1])
    west_w = 0.5 * (centre + padded[1:-1, :-2])
    east_w = 0.5 * (centre + padded[1:-1, 2:])
    return north_w, south_w, west_w, east_w


def jacobi_step(source, padded, weights, divisor):
    summed = source + weights[0][..., None] * padded[:-2, 1:-1]
    summed = summed + weights[1][..., None] * padded[2:, 1:-1]
    summed = summed + weights[2][..., None] * padded[1:-1, :-2]
    summed = summed + weights[3][..., None] * padded[1:-1, 2:]
    return summed / divisor[..., None]


def reference(operator_t, data_columns, noise_var, class_map, diffusion_table, kappa_table):
    diffusion = lookup(class_map, diffusion_table)
    reaction = lookup(class_map, kappa_table)
    weights = edge_weights(jnp.pad(diffusion, 1))
    divisor = reaction + weights[0] + weights[1] + weights[2] + weights[3]
    flattened = operator_t.reshape(NX * NY, NDATA)
    source = jnp.dot(flattened, data_columns, preferred_element_type=jnp.float32).reshape(NX, NY, K)
    iterate = source / divisor[..., None]
    for repeat in range(ITERS):
        padded = jnp.pad(iterate, ((1, 1), (1, 1), (0, 0)))
        iterate = jacobi_step(source, padded, weights, divisor)
    smooth = iterate.astype(jnp.bfloat16).reshape(NX * NY, K)
    forward = lax.dot_general(flattened, smooth, (((0,), (0,)), ((), ())), preferred_element_type=jnp.float32)
    return forward + noise_var[:, None] * data_columns.astype(jnp.float32), iterate
```

```python
import functools
import jax
import jax.numpy as jnp
from jax import lax
from jax.experimental import pallas as pl
from jax.experimental.pallas import tpu as pltpu
from jax.sharding import PartitionSpec as P

ITERS = 8
MESH = pl.DeviceIdType.MESH


def up8(n):
    return -(-n // 8) * 8


class Place:
    def __init__(self, dims):
        self.Y, self.X, self.Z = dims
        gx, gy = lax.axis_index("gx"), lax.axis_index("gy")
        self.y, self.x = gx // self.X, gx % self.X
        self.z, self.core = gy // 2, gy % 2
        self.n = {"x": self.X, "y": self.Y, "z": self.Z}
        self.at = {"x": self.x, "y": self.y, "z": self.z}

    def device(self, **moved):
        c = {**self.at, "core": self.core, **moved}
        return (c["y"] * self.X + c["x"], c["z"] * 2 + c["core"])

    def ahead(self, axis, d):
        return (self.at[axis] + d) % self.n[axis]

    def peers(self):
        found = [self.device(core=1 - self.core)]
        for axis in "xyz":
            found += [self.device(**{axis: self.ahead(axis, d)}) for d in range(1, self.n[axis])]
        return found

    def barrier(self):
        ready = pltpu.get_barrier_semaphore()
        peers = self.peers()
        for peer in peers:
            pl.semaphore_signal(ready, inc=1, device_id=peer, device_id_type=MESH)
        pl.semaphore_wait(ready, len(peers))


def remote(src, dst, send, recv, device):
    return pltpu.make_async_remote_copy(
        src_ref=src, dst_ref=dst, send_sem=send, recv_sem=recv, device_id=device, device_id_type=MESH
    )


LEVELS = 32767.0


def encode(value, coded, scale):
    top = jnp.maximum(jnp.max(jnp.abs(value), axis=-2, keepdims=True), 1e-30)
    coded[...] = jnp.round(value * (LEVELS / top)).astype(jnp.int32).astype(jnp.int16)
    scale[...] = jnp.broadcast_to(top * (1.0 / LEVELS), scale.shape)


def decode(coded, scale):
    top = scale[...]
    return coded[...].astype(jnp.int32).astype(jnp.float32) * top[..., :1, :]


def gather_kernel(dims, mine, full, own_sem, sz, rz, s1, r1, s2, r2, ss, rs):
    here = Place(dims)
    Y, X, Z = dims
    me = here.core
    sib = here.device(core=1 - me)
    home = full.at[here.y, here.x, here.z, me]
    copy = pltpu.make_async_copy(mine, home, own_sem)
    copy.start()
    here.barrier()
    copies = []
    for d in range(1, Z):
        sent = remote(mine, home, sz.at[d - 1], rz.at[d - 1], here.device(z=here.ahead("z", d)))
        sent.start()
        copies.append(sent)
    copy.wait()
    for c in (0, 1):

        @pl.when(me == c)
        def _():
            near, far = "xy"[c], "yx"[c]
            n1, n2 = here.n[near], here.n[far]
            sent_here = []

            def block(d, e, f, core):
                x, y = ((e, f), (f, e))[c]
                return full.at[here.ahead("y", -y), here.ahead("x", -x), here.ahead("z", -d), core]

            def share_number(d, e, f):
                x, y = ((e, f), (f, e))[c]
                return (d * X + x) * Y + y

            def start(*what):
                sent = remote(*what)
                sent.start()
                sent_here.append(sent)

            def arrived(ref, send, recv):
                remote(ref, ref, send, recv, sib).wait_recv()

            def to_far(held, d, e):
                for f in range(1, n2):
                    k = (d * n1 + e) * n2 + f
                    start(
                        held, held, s2.at[k], r2.at[k], here.device(**{far: here.ahead(far, f)})
                    )

            def to_sibling(held, d, e, f):
                k = share_number(d, e, f)
                start(held, held, ss.at[k], rs.at[k], sib)

            for d in range(Z):
                held = block(d, 0, 0, c)
                if d:
                    arrived(held, sz.at[d - 1], rz.at[d - 1])
                for e in range(1, n1):
                    k = d * n1 + e
                    start(
                        held, held, s1.at[k], r1.at[k], here.device(**{near: here.ahead(near, e)})
                    )
                to_far(held, d, 0)
                to_sibling(held, d, 0, 0)
            for d in range(Z):
                for e in range(1, n1):
                    held = block(d, e, 0, c)
                    arrived(held, s1.at[d * n1 + e], r1.at[d * n1 + e])
                    to_far(held, d, e)
                    to_sibling(held, d, e, 0)
            for e in range(n1):
                for d in range(Z):
                    for f in range(1, n2):
                        held = block(d, e, f, c)
                        k = (d * n1 + e) * n2 + f
                        arrived(held, s2.at[k], r2.at[k])
                        to_sibling(held, d, e, f)
            for d in range(Z):
                for e in range(n1):
                    for f in range(n2):
                        k = share_number(d, e, f)
                        arrived(block(d, e, f, 1 - c), ss.at[k], rs.at[k])
            for sent in sent_here:
                sent.wait_send()

    for sent in copies:
        sent.wait_send()


def gather(dims, block):
    Y, X, Z = dims
    dma = pltpu.SemaphoreType.DMA
    widest = max(X, Y)
    return pl.pallas_call(
        functools.partial(gather_kernel, dims),
        out_shape=jax.ShapeDtypeStruct((Y, X, Z, 2) + block.shape, block.dtype),
        in_specs=[pl.BlockSpec(memory_space=pltpu.VMEM)],
        out_specs=pl.BlockSpec(memory_space=pltpu.VMEM),
        scratch_shapes=[dma]
        + [dma((max(Z - 1, 1),))] * 2
        + [dma((Z * widest,))] * 2
        + [dma((X * Y * Z,))] * 4,
        compiler_params=pltpu.CompilerParams(
            collective_id=0, has_side_effects=True, vmem_limit_bytes=16 << 20
        ),
    )(block)


def scatter_kernel(dims, starts, H, fused, *refs):
    if fused:
        operator, field, out, *refs = refs
    else:
        part, out, *refs = refs
    total, r0, r1x, r1y, r2x, r2y, r3 = refs[:7]
    f1x, f1y, f2x, f2y, f3, q1, q2, q3, c1, c2, c3 = refs[7:18]
    refs = refs[18:]
    if fused:
        part, wide, *refs = refs
    here = Place(dims)
    Y, X, Z = dims
    pair = part.shape[3]
    me = here.core
    sib = here.device(core=1 - me)
    s0, g0, s1, g1, s2, g2, s3, g3, t1, h1, t2, h2, t3, h3 = refs
    ready = pltpu.get_barrier_semaphore()
    peers = here.peers()
    for peer in peers:
        pl.semaphore_signal(ready, inc=1, device_id=peer, device_id_type=MESH)
    order = [(dy, dx) for dy in [*range(1, Y), 0] for dx in [*range(1, X), 0]]
    order.sort(key=lambda step: (step[0] == 0) + (step[1] == 0))
    for number, (dy, dx) in enumerate(order):
        y, x = here.ahead("y", dy), here.ahead("x", dx)
        if fused:
            span = wide.shape[0]
            row = (y * X + x) * (Z * pair)
            base = jnp.minimum(row // 128, (operator.shape[1] - span) // 128) * 128
            wide[...] = lax.dot_general(
                operator[:, pl.ds(pl.multiple_of(base, 128), span)],
                field[...],
                (((0,), (0,)), ((), ())),
                preferred_element_type=jnp.float32,
            )
            for z in range(Z):
                part[y, x, z] = wide[pl.ds(pl.multiple_of(row - base + z * pair, 8), pair), :]
        if number == 0:
            pl.semaphore_wait(ready, len(peers))
        for c in (0, 1):

            @pl.when(me == c)
            def _():
                remote(
                    part.at[y, x, :, pl.ds(starts[1 - c], H), :],
                    r0.at[y, x],
                    s0.at[number],
                    g0.at[number],
                    sib,
                ).start()

    for c in (0, 1):

        @pl.when(me == c)
        def _():
            near, far = "xy"[c], "yx"[c]
            r1, r2 = (r1x, r2y) if c == 0 else (r1y, r2x)
            f1, f2 = (f1x, f2y) if c == 0 else (f1y, f2x)
            n1, n2 = here.n[near], here.n[far]
            sent_here = []

            def send(*what):
                sent = remote(*what)
                sent.start()
                sent_here.append(sent)

            sorted_steps = sorted(
                enumerate(order), key=lambda item: (item[1][1 - c] == 0, item[0])
            )
            for number, (dy, dx) in sorted_steps:
                y, x = here.ahead("y", dy), here.ahead("x", dx)
                arrived = r0.at[y, x]
                remote(arrived, arrived, s0.at[number], g0.at[number], sib).wait_recv()
                value = part[y, x, :, pl.ds(starts[c], H), :] + arrived[...]
                d = (dx, dy)[c]
                if d:
                    encode(value, q1.at[number], c1.at[number])
                    peer, slot = here.device(**{near: (x, y)[c]}), (d - 1, (y, x)[c])
                    send(q1.at[number], r1.at[slot], s1.at[number], g1.at[number], peer)
                    send(c1.at[number], f1.at[slot], t1.at[number], h1.at[number], peer)
                else:
                    total[y, x] = value
            for d2 in [*range(1, n2), 0]:
                index = here.ahead(far, d2)
                held = total.at[(index, here.x) if c == 0 else (here.y, index)]
                value = held[...]
                for d in range(1, n1):
                    number = order.index((d2, d) if c == 0 else (d, d2))
                    back, by = r1.at[d - 1, index], f1.at[d - 1, index]
                    remote(back, back, s1.at[number], g1.at[number], sib).wait_recv()
                    remote(by, by, t1.at[number], h1.at[number], sib).wait_recv()
                    value = value + decode(back, by)
                if d2:
                    encode(value, q2.at[d2 - 1], c2.at[d2 - 1])
                    peer = here.device(**{far: index})
                    send(q2.at[d2 - 1], r2.at[d2 - 1], s2.at[d2 - 1], g2.at[d2 - 1], peer)
                    send(c2.at[d2 - 1], f2.at[d2 - 1], t2.at[d2 - 1], h2.at[d2 - 1], peer)
                else:
                    held[...] = value
            held = total.at[here.y, here.x]
            value = held[...]
            for e in range(1, n2):
                back, by = r2.at[e - 1], f2.at[e - 1]
                remote(back, back, s2.at[e - 1], g2.at[e - 1], sib).wait_recv()
                remote(by, by, t2.at[e - 1], h2.at[e - 1], sib).wait_recv()
                value = value + decode(back, by)
            held[...] = value
            for d in range(1, Z):
                index = here.ahead("z", d)
                encode(held[index], q3.at[d - 1], c3.at[d - 1])
                peer = here.device(z=index)
                send(q3.at[d - 1], r3.at[d - 1], s3.at[d - 1], g3.at[d - 1], peer)
                send(c3.at[d - 1], f3.at[d - 1], t3.at[d - 1], h3.at[d - 1], peer)
            value = held[here.z]
            for d in range(1, Z):
                back, by = r3.at[d - 1], f3.at[d - 1]
                remote(back, back, s3.at[d - 1], g3.at[d - 1], sib).wait_recv()
                remote(by, by, t3.at[d - 1], h3.at[d - 1], sib).wait_recv()
                value = value + decode(back, by)
            out[...] = value
            for sent in sent_here:
                sent.wait_send()
            for number, (dy, dx) in enumerate(order):
                y, x = here.ahead("y", dy), here.ahead("x", dx)
                remote(
                    part.at[y, x, :, pl.ds(starts[1 - c], H), :],
                    r0.at[y, x],
                    s0.at[number],
                    g0.at[number],
                    sib,
                ).wait_send()


def scatter(dims, operator, field, rows):
    Y, X, Z = dims
    points, data_rows = operator.shape
    columns = field.shape[1]
    start = rows // 8 * 8
    H = max(up8(rows), up8(2 * rows) - start)
    pair = max(H + start, 2 * rows)
    group = Z * pair
    span = -(-(group + 127) // 128) * 128
    fused = pair == 2 * rows and pair % 8 == 0 and data_rows % 128 == 0 and span <= data_rows
    dma = pltpu.SemaphoreType.DMA
    widest = max(X, Y)
    f32, i16 = jnp.float32, jnp.int16

    def held(*lead, rows=H, kind=f32):
        return pltpu.VMEM(tuple(max(n, 1) for n in lead) + (rows, columns), kind)

    def lanes(kind, rows):
        return [
            held(X - 1, Y, Z, rows=rows, kind=kind),
            held(Y - 1, X, Z, rows=rows, kind=kind),
            held(X - 1, Z, rows=rows, kind=kind),
            held(Y - 1, Z, rows=rows, kind=kind),
            held(Z - 1, rows=rows, kind=kind),
        ]

    def out_going(kind, rows):
        return [
            held(X * Y, Z, rows=rows, kind=kind),
            held(widest - 1, Z, rows=rows, kind=kind),
            held(Z - 1, rows=rows, kind=kind),
        ]

    scratch = [held(Y, X, Z), held(Y, X, Z)]
    scratch += lanes(i16, H) + lanes(f32, 8) + out_going(i16, H) + out_going(f32, 8)
    if fused:
        given = (operator, field)
        scratch += [pltpu.VMEM((Y, X, Z, pair, columns), f32), pltpu.VMEM((span, columns), f32)]
    else:
        part = lax.dot_general(
            operator, field, (((0,), (0,)), ((), ())), preferred_element_type=f32
        ).reshape(Y, X, Z, 2 * rows, columns)
        given = (jnp.pad(part, ((0, 0),) * 3 + ((0, pair - 2 * rows), (0, 0))),)
    vmem = pl.BlockSpec(memory_space=pltpu.VMEM)
    stage2, stage3 = max(widest - 1, 1), max(Z - 1, 1)
    out = pl.pallas_call(
        functools.partial(scatter_kernel, dims, (0, start), H, fused),
        out_shape=jax.ShapeDtypeStruct((H, columns), f32),
        in_specs=[vmem] * len(given),
        out_specs=vmem,
        scratch_shapes=scratch
        + [dma((X * Y,))] * 4
        + [dma((stage2,))] * 2
        + [dma((stage3,))] * 2
        + [dma((X * Y,))] * 2
        + [dma((stage2,))] * 2
        + [dma((stage3,))] * 2,
        compiler_params=pltpu.CompilerParams(
            collective_id=1, has_side_effects=True, vmem_limit_bytes=40 << 20
        ),
    )(*given)
    core = lax.axis_index("gy") % 2
    return jnp.where(core == 0, out[:rows], out[rows - start : 2 * rows - start])


def smooth_kernel(
    counts, start, coef, prior, smooth, s, u, v, up_out, down_out, up_in, down_in, local, send, recv
):
    rows, cols, width = start.shape
    m = ITERS
    gx, gy = lax.axis_index("gx"), lax.axis_index("gy")
    count_x, count_y = counts
    sides = {
        "n": (gx > 0, (gx - 1, gy), gx < count_x - 1),
        "s": (gx < count_x - 1, (gx + 1, gy), gx > 0),
        "w": (gy > 0, (gx, gy - 1), gy < count_y - 1),
        "e": (gy < count_y - 1, (gx, gy + 1), gy > 0),
    }
    inner_r, inner_c = pl.ds(m, rows), pl.ds(m, cols)
    low, high_r, high_c = pl.ds(0, m), pl.ds(m + rows, m), pl.ds(m + cols, m)
    home = pltpu.make_async_copy(start, s.at[inner_r, inner_c], local)
    home.start()
    for side, where in (("n", (low, slice(None))), ("s", (high_r, slice(None)))):

        @pl.when(jnp.logical_not(sides[side][0]))
        def _():
            s[where] = jnp.zeros((m, cols + 2 * m, width), jnp.float32)

    for side, where in (("w", low), ("e", high_c)):

        @pl.when(jnp.logical_not(sides[side][0]))
        def _():
            s[:, where] = jnp.zeros((rows + 2 * m, m, width), jnp.float32)

    ready = pltpu.get_barrier_semaphore()
    for has, peer, _ in sides.values():

        @pl.when(has)
        def _():
            pl.semaphore_signal(ready, inc=1, device_id=peer, device_id_type=MESH)

    up_out[...] = start[1:m].astype(jnp.bfloat16)
    down_out[...] = start[rows - m : rows - 1].astype(jnp.bfloat16)
    pl.semaphore_wait(ready, sum(jnp.where(has, 1, 0) for has, _, _ in sides.values()))

    first = (
        (0, "n", start.at[pl.ds(0, 1)], s.at[pl.ds(m + rows, 1), inner_c]),
        (1, "s", start.at[pl.ds(rows - 1, 1)], s.at[pl.ds(m - 1, 1), inner_c]),
        (2, "n", up_out, up_in),
        (3, "s", down_out, down_in),
        (4, "w", start.at[:, pl.ds(0, m)], s.at[inner_r, high_c]),
        (5, "e", start.at[:, pl.ds(cols - m, m)], s.at[inner_r, low]),
    )
    second = (
        (6, "w", s.at[low, pl.ds(m, m)], s.at[low, high_c]),
        (7, "w", s.at[high_r, pl.ds(m, m)], s.at[high_r, high_c]),
        (8, "e", s.at[low, pl.ds(cols, m)], s.at[low, low]),
        (9, "e", s.at[high_r, pl.ds(cols, m)], s.at[high_r, low]),
    )

    def each(group, what):
        for number, side, src, dst in group:
            has, peer, gets = sides[side]
            copy = remote(src, dst, send.at[number], recv.at[number], peer)

            @pl.when(gets if what == "wait_recv" else has)
            def _():
                getattr(copy, what)()

    each(first, "start")
    home.wait()
    each(first, "wait_recv")

    @pl.when(sides["s"][0])
    def _():
        s[pl.ds(m + rows + 1, m - 1), inner_c] = up_in[...].astype(jnp.float32)

    @pl.when(sides["n"][0])
    def _():
        s[pl.ds(0, m - 1), inner_c] = down_in[...].astype(jnp.float32)

    each(second, "start")
    each(second, "wait_recv")
    each(first, "wait_send")
    each(second, "wait_send")

    held = [s, u, v]
    wide = cols + 2 * m
    for step in range(1, ITERS + 1):
        old = s if step == 1 else held[1 + step % 2]
        new = held[1 + (step + 1) % 2]
        last = step == ITERS

        @pl.loop(step, rows + 2 * m - step)
        def _(r):
            for g in range(width // 128):
                lanes = pl.ds(g * 128, 128)
                centre = old[r, :, lanes]
                value = s[r, :, lanes] + coef[0, r] * old[r - 1, :, lanes]
                value = value + coef[1, r] * old[r + 1, :, lanes]
                value = value + coef[2, r] * pltpu.roll(centre, 1, 0)
                value = value + coef[3, r] * pltpu.roll(centre, wide - 1, 0)
                if last:
                    prior[r - m, :, lanes] = value[m : m + cols]
                    smooth[r - m, :, lanes] = value[m : m + cols].astype(jnp.bfloat16)
                else:
                    new[r, :, lanes] = value


def smoothed(start, coef):
    rows, cols, width = start.shape
    m = ITERS
    whole = pltpu.VMEM((rows + 2 * m, cols + 2 * m, width), jnp.float32)
    strip = pltpu.VMEM((m - 1, cols, width), jnp.bfloat16)
    dma = pltpu.SemaphoreType.DMA
    vmem = pl.BlockSpec(memory_space=pltpu.VMEM)
    return pl.pallas_call(
        functools.partial(smooth_kernel, (lax.axis_size("gx"), lax.axis_size("gy"))),
        out_shape=(
            jax.ShapeDtypeStruct(start.shape, jnp.float32),
            jax.ShapeDtypeStruct(start.shape, jnp.bfloat16),
        ),
        in_specs=[vmem, vmem],
        out_specs=(vmem, vmem),
        scratch_shapes=[whole] * 3 + [strip] * 4 + [dma, dma((10,)), dma((10,))],
        compiler_params=pltpu.CompilerParams(
            collective_id=2, has_side_effects=True, vmem_limit_bytes=40 << 20
        ),
    )(start, coef)


def mesh_dims():
    gx, gy = lax.axis_size("gx"), lax.axis_size("gy")
    return (gx // 2, 2, gy // 2)


def lookup(classes, entries):
    onehot = (classes[..., None] == jnp.arange(entries.shape[0], dtype=jnp.int32)).astype(
        jnp.float32
    )
    return jnp.sum(onehot * entries, axis=-1)


def edge_weights(padded):
    centre = padded[1:-1, 1:-1]
    north_w = 0.5 * (centre + padded[:-2, 1:-1])
    south_w = 0.5 * (centre + padded[2:, 1:-1])
    west_w = 0.5 * (centre + padded[1:-1, :-2])
    east_w = 0.5 * (centre + padded[1:-1, 2:])
    return (north_w, south_w, west_w, east_w)


def local(operator_t, data_columns, noise_var, class_map, diffusion_table, kappa_table):
    tile_rows, tile_cols, data_rows = operator_t.shape
    count, width = data_columns.shape
    gx_size, gy_size = lax.axis_size("gx"), lax.axis_size("gy")
    flattened = operator_t.reshape(tile_rows * tile_cols, data_rows)
    points = tile_rows * tile_cols
    extra = -(-points // width)
    classes = jnp.pad(class_map.reshape(points).astype(jnp.bfloat16), (0, extra * width - points))
    block = jnp.concatenate([data_columns, classes.reshape(extra, width)], axis=0)
    full = gather(mesh_dims(), block)
    data = full[..., :count, :].reshape(data_rows, width)
    classes = full[..., count:, :].reshape(gx_size, gy_size, extra * width)[..., :points]
    classes = classes.reshape(gx_size, gy_size, tile_rows, tile_cols).astype(jnp.int32)
    classes = classes.transpose(0, 2, 1, 3).reshape(gx_size * tile_rows, gy_size * tile_cols)
    edge = ITERS + 1
    classes = jnp.pad(classes, edge, constant_values=-1)
    window = lax.dynamic_slice(
        classes,
        (lax.axis_index("gx") * tile_rows, lax.axis_index("gy") * tile_cols),
        (tile_rows + 2 * edge, tile_cols + 2 * edge),
    )
    inside = (window >= 0)[1:-1, 1:-1]
    weights = edge_weights(lookup(window, diffusion_table))
    reaction = lookup(window, kappa_table)[1:-1, 1:-1]
    divisor = jnp.where(inside, reaction + weights[0] + weights[1] + weights[2] + weights[3], 1.0)
    coef = jnp.stack([jnp.where(inside, w / divisor, 0.0) for w in weights])
    coef = jnp.broadcast_to(coef[..., None], coef.shape + (128,))
    source = jnp.dot(flattened, data, preferred_element_type=jnp.float32)
    tile_divisor = divisor[ITERS:-ITERS, ITERS:-ITERS]
    start = source.reshape(tile_rows, tile_cols, width) / tile_divisor[..., None]
    iterate, smooth = smoothed(start, coef)
    forward = scatter(mesh_dims(), flattened, smooth.reshape(points, width), count)
    return (forward + noise_var[:, None] * data_columns.astype(jnp.float32), iterate)


def solution(mesh):
    placed = (P("gx", "gy", None), P(("gx", "gy"), None), P(("gx", "gy")), P("gx", "gy"), P(), P())
    return jax.shard_map(
        local,
        mesh=mesh,
        in_specs=placed,
        out_specs=(P(("gx", "gy"), None), P("gx", "gy", None)),
        check_vma=False,
    )
```

```python
import functools
import jax
import jax.numpy as jnp
from jax import lax
from jax.experimental import pallas as pl
from jax.experimental.pallas import tpu as pltpu
from jax.sharding import PartitionSpec as P

ITERS = 8
LANES = 128
LEVELS = 32767.0
MESH = pl.DeviceIdType.MESH


def up8(n):
    return -(-n // 8) * 8


def remote(src, dst, send, recv, device):
    return pltpu.make_async_remote_copy(
        src_ref=src, dst_ref=dst, send_sem=send, recv_sem=recv, device_id=device, device_id_type=MESH
    )


def top_of(value, axes):
    return jnp.maximum(jnp.max(jnp.abs(value), axis=axes, keepdims=True), 1e-30)


def coded(value, top):
    return jnp.round(value * (LEVELS / top)).astype(jnp.int32).astype(jnp.int16)


def decoded(codes, scale):
    return codes.astype(jnp.int32).astype(jnp.float32) * scale


def block_kernel(
    dims, counts, start_row, H,
    mine, classes, diffusion_table, kappa_table, operator_hbm,
    out, prior,
    operator, full, stage, data, near_classes, coef, inverse,
    s, u, v, q_out, q_scale, q_in, q_in_scale, smooth,
    flat, wide, sib_in, xy_q, xy_c, xy_r, xy_f, z_q, z_c, z_r, z_f, own,
    op_sem, cls_s, cls_r, gz_s, gz_r, gx_s, gx_r, gs_s, gs_r,
    hq_s, hq_r, hc_s, hc_r, he_s, he_r, hk_s, hk_r,
    rs_s, rs_r, rq_s, rq_r, rc_s, rc_r, zq_s, zq_r, zc_s, zc_r,
):
    Y, X, Z = dims
    m = ITERS
    chunks = s.shape[0]
    rows, cols = prior.shape[0], prior.shape[1]
    count = mine.shape[0]
    pair = 2 * count
    chips = Y * X * Z
    count_x, count_y = counts
    gx, gy = lax.axis_index("gx"), lax.axis_index("gy")
    y, x, z, me = gx // X, gx % X, gy // 2, gy % 2
    offsets = [(dy, dx) for dy in range(Y) for dx in range(X)][1:]
    offsets.sort(key=lambda d: (d[0] != 0) + (d[1] != 0))

    def device(y=y, x=x, z=z, core=me):
        return (y * X + x, z * 2 + core)

    sib = device(core=1 - me)
    z_peers = [device(z=(z + d) % Z) for d in range(1, Z)]
    xy_peers = [device(y=(y + dy) % Y, x=(x + dx) % X) for dy, dx in offsets]
    around = [(dr, dc) for dr in (-1, 0, 1) for dc in (-1, 0, 1) if (dr, dc) != (0, 0)]

    def exists(dr, dc):
        has = None
        for d, at, n in ((dr, gx, count_x), (dc, gy, count_y)):
            if d:
                ok = at > 0 if d < 0 else at < n - 1
                has = ok if has is None else has & ok
        return has

    def lanes(g):
        return pl.ds(g * LANES, LANES)

    pending = []

    def send(src, dst, sends, recvs, peer):
        copy = remote(src, dst, sends, recvs, peer)
        copy.start()
        pending.append((None, copy))

    def send_if(has, src, dst, sends, recvs, peer):
        copy = remote(src, dst, sends, recvs, peer)

        @pl.when(has)
        def _():
            copy.start()

        pending.append((has, copy))

    def arrived(ref, sends, recvs):
        remote(ref, ref, sends, recvs, sib).wait_recv()

    load = pltpu.make_async_copy(operator_hbm, operator, op_sem)
    load.start()
    for g in range(chunks):
        full[g, y, x, me, z] = mine[:, g * LANES : (g + 1) * LANES]

    wide_rows, wide_cols = rows + 2 * m, cols + 2 * m
    for (dr, dc), where in (
        ((-1, 0), (pl.ds(0, m), pl.ds(0, wide_cols))),
        ((1, 0), (pl.ds(m + rows, m), pl.ds(0, wide_cols))),
        ((0, -1), (pl.ds(0, wide_rows), pl.ds(0, m))),
        ((0, 1), (pl.ds(0, wide_rows), pl.ds(m + cols, m))),
    ):

        @pl.when(jnp.logical_not(exists(dr, dc)))
        def _():
            for g in range(chunks):
                s[g, where[0], where[1]] = jnp.zeros(
                    (where[0].size, where[1].size, LANES), jnp.float32
                )

    ready = pltpu.get_barrier_semaphore()
    for peer in [sib, *z_peers, *xy_peers]:
        pl.semaphore_signal(ready, inc=1, device_id=peer, device_id_type=MESH)
    total = 1 + len(z_peers) + len(xy_peers)
    for dr, dc in around:

        @pl.when(exists(dr, dc))
        def _():
            pl.semaphore_signal(
                ready, inc=1, device_id=(gx + dr, gy + dc), device_id_type=MESH
            )

        total = total + jnp.where(exists(dr, dc), 1, 0)
    pl.semaphore_wait(ready, total)

    for i, (dr, dc) in enumerate(around):
        send_if(
            exists(dr, dc), classes, near_classes.at[7 - i], cls_s.at[i], cls_r.at[7 - i],
            (gx + dr, gy + dc),
        )
    for g in range(chunks):
        home = full.at[g, y, x, me, z]
        for d in range(1, Z):
            send(home, home, gz_s.at[g, d - 1], gz_r.at[g, d - 1], z_peers[d - 1])
        for j, peer in enumerate(xy_peers):
            send(home, home, gx_s.at[g, 0, j], gx_r.at[g, 0, j], peer)

    for i, (dr, dc) in enumerate(around):
        has = exists(dr, dc)

        @pl.when(has)
        def _():
            arrived(near_classes.at[i], cls_s.at[i], cls_r.at[i])

        @pl.when(jnp.logical_not(has))
        def _():
            near_classes[i] = jnp.full((rows, LANES), -1, jnp.int32)

    reach = m + 1
    lane = lax.broadcasted_iota(jnp.int32, (rows, LANES), 1)
    window = []
    for dr in (-1, 0, 1):
        west, centre, east = [
            near_classes[around.index((dr, dc))] if (dr, dc) != (0, 0) else classes[...]
            for dc in (-1, 0, 1)
        ]
        west = pltpu.roll(west, LANES - (cols - reach), 1)
        centre = pltpu.roll(centre, reach, 1)
        east = pltpu.roll(east, reach + cols, 1)
        line = jnp.where(lane < reach, west, jnp.where(lane < reach + cols, centre, east))
        window.append(jnp.where(lane < 2 * reach + cols, line, -1))
    window = jnp.concatenate(window, axis=0)
    tall = 3 * rows
    diffusion = jnp.zeros((tall, LANES), jnp.float32)
    reaction = jnp.zeros((tall, LANES), jnp.float32)
    for k in range(diffusion_table.shape[0]):
        hit = window == k
        diffusion = jnp.where(hit, diffusion_table[k], diffusion)
        reaction = jnp.where(hit, kappa_table[k], reaction)
    inside = window >= 0
    weights = [
        0.5 * (diffusion + pltpu.roll(diffusion, shift, axis))
        for shift, axis in ((1, 0), (tall - 1, 0), (1, 1), (LANES - 1, 1))
    ]
    divisor = jnp.where(
        inside, reaction + weights[0] + weights[1] + weights[2] + weights[3], 1.0
    )

    def upright(values):
        values = pltpu.roll(values, LANES - 1, 1)[rows - m : rows - m + wide_rows]
        padded = jnp.concatenate(
            [values, jnp.zeros((LANES - wide_rows, LANES), jnp.float32)], axis=0
        )
        return padded.T

    for i, w in enumerate(weights):
        turned = upright(jnp.where(inside, w / divisor, 0.0))
        for r in range(wide_rows):
            coef[i, r] = jnp.broadcast_to(turned[:wide_cols, r : r + 1], (wide_cols, LANES))
    turned = upright(1.0 / divisor)
    for r in range(rows):
        inverse[r] = jnp.broadcast_to(turned[m : m + cols, m + r : m + r + 1], (cols, LANES))

    def held(g, d, core=me):
        return full.at[g, y, x, core, (z - d) % Z]

    def to_sibling(g, j):
        dy, dx = ([(0, 0)] + offsets)[j]
        group = full.at[g, (y - dy) % Y, (x - dx) % X, me]
        send(group, group, gs_s.at[g, j], gs_r.at[g, j], sib)

    def gather_z(g):
        for d in range(1, Z):
            block = held(g, d)
            arrived(block, gz_s.at[g, d - 1], gz_r.at[g, d - 1])
            for j, peer in enumerate(xy_peers):
                send(block, block, gx_s.at[g, d, j], gx_r.at[g, d, j], peer)
        to_sibling(g, 0)

    def gather_xy(g):
        for j, (dy, dx) in enumerate(offsets):
            for d in range(Z):
                block = full.at[g, (y - dy) % Y, (x - dx) % X, me, (z - d) % Z]
                arrived(block, gx_s.at[g, d, j], gx_r.at[g, d, j])
            to_sibling(g, j + 1)

    def sources(g):
        for j, (dy, dx) in enumerate([(0, 0)] + offsets):
            group = full.at[g, (y - dy) % Y, (x - dx) % X, 1 - me]
            arrived(group, gs_s.at[g, j], gs_r.at[g, j])
        number = 0
        for yy in range(Y):
            for xx in range(X):
                for zz in range(Z):
                    for core in (0, 1):
                        stage[pl.ds(number * count, count), :] = full[
                            g, yy, xx, core, zz
                        ].astype(jnp.float32)
                        number += 1
        data[...] = stage[...].astype(jnp.bfloat16)
        source = jnp.dot(operator[...], data[...], preferred_element_type=jnp.float32)
        tile = source.reshape(rows, cols, LANES) * inverse[...]
        s[g, pl.ds(m, rows), pl.ds(m, cols)] = tile
        top = top_of(tile, (0, 1))
        q_out[g] = coded(tile, top)
        q_scale[g] = jnp.broadcast_to(top[0] * (1.0 / LEVELS), (8, LANES))

    north, south, west, east = (-1, 0), (1, 0), (0, -1), (0, 1)

    def peer_of(d):
        return (gx + d[0], gy + d[1])

    def halo_send(g):
        for i, (d, at) in enumerate(((north, 0), (south, rows - m))):
            has = exists(*d)
            send_if(
                has, q_out.at[g, pl.ds(at, m)], q_in.at[g, i], hq_s.at[g, i], hq_r.at[g, i],
                peer_of(d),
            )
            send_if(
                has, q_scale.at[g], q_in_scale.at[g, i], hc_s.at[g, i], hc_r.at[g, i], peer_of(d)
            )
        inner = pl.ds(m, rows)
        for i, (d, src, dst) in enumerate(((west, m, m + cols), (east, cols, 0))):
            send_if(
                exists(*d), s.at[g, inner, pl.ds(src, m)], s.at[g, inner, pl.ds(dst, m)],
                he_s.at[g, i], he_r.at[g, i], peer_of(d),
            )

    def halo_recv(g):
        for i, (d, at) in enumerate(((south, m + rows), (north, 0))):

            @pl.when(exists(*d))
            def _():
                arrived(q_in.at[g, i], hq_s.at[g, i], hq_r.at[g, i])
                arrived(q_in_scale.at[g, i], hc_s.at[g, i], hc_r.at[g, i])
                s[g, pl.ds(at, m), pl.ds(m, cols)] = decoded(
                    q_in[g, i], q_in_scale[g, i][:1][None]
                )

        for i, (d, src, dst) in enumerate(((west, m, m + cols), (east, cols, 0))):
            for k, at in enumerate((0, m + rows)):
                send_if(
                    exists(*d), s.at[g, pl.ds(at, m), pl.ds(src, m)],
                    s.at[g, pl.ds(at, m), pl.ds(dst, m)],
                    hk_s.at[g, i, k], hk_r.at[g, i, k], peer_of(d),
                )

    def halo_sides(g):
        for i, (d, dst) in enumerate(((east, m + cols), (west, 0))):

            @pl.when(exists(*d))
            def _():
                block = s.at[g, pl.ds(m, rows), pl.ds(dst, m)]
                arrived(block, he_s.at[g, i], he_r.at[g, i])
                for k, at in enumerate((0, m + rows)):
                    block = s.at[g, pl.ds(at, m), pl.ds(dst, m)]
                    arrived(block, hk_s.at[g, i, k], hk_r.at[g, i, k])

    def sweeps(g):
        turns = [u, v]
        fixed = s.at[g]
        for step in range(1, m + 1):
            old = fixed if step == 1 else turns[step % 2]
            new = turns[(step + 1) % 2]
            last = step == m

            @pl.loop(step, wide_rows - step)
            def _(r):
                centre = old[r]
                value = fixed[r] + coef[0, r] * old[r - 1]
                value = value + coef[1, r] * old[r + 1]
                value = value + coef[2, r] * pltpu.roll(centre, 1, 0)
                value = value + coef[3, r] * pltpu.roll(centre, wide_cols - 1, 0)
                if last:
                    done = value[m : m + cols]
                    prior[r - m, :, lanes(g)] = done
                    at = pl.multiple_of((r - m) * cols, cols)
                    smooth[pl.ds(at, cols), :] = done.astype(jnp.bfloat16)
                else:
                    new[r] = value

    mine_rows = pl.ds(pl.multiple_of(me * start_row, 8), H)
    other_rows = pl.ds(pl.multiple_of((1 - me) * start_row, 8), H)
    groups = [*offsets, (0, 0)]

    def group_at(j):
        dy, dx = groups[j]
        return ((y + dy) % Y) * X + (x + dx) % X

    def forward(g):
        partial = lax.dot_general(
            operator[...], smooth[...], (((0,), (0,)), ((), ())),
            preferred_element_type=jnp.float32,
        )
        if pair % 8 == 0:
            wide[g] = partial.reshape(Y * X, Z, pair, LANES)
        else:
            flat[...] = partial
            for k in range(chips):
                wide[g, k // Z, k % Z, pl.ds(0, pair)] = flat[pl.ds(k * pair, pair)]
                rest = wide.shape[3] - pair
                wide[g, k // Z, k % Z, pl.ds(pair, rest)] = jnp.zeros((rest, LANES), jnp.float32)
        for j in range(len(groups)):
            k = group_at(j)
            send(
                wide.at[g, k, :, other_rows], sib_in.at[g, k], rs_s.at[g, j], rs_r.at[g, j], sib
            )

    def pair_sum(g, j, zz):
        k = group_at(j)
        return wide[g, k, zz, mine_rows] + sib_in[g, k, zz]

    def scatter_xy(g):
        for j, peer in enumerate(xy_peers):
            k = group_at(j)
            arrived(sib_in.at[g, k], rs_s.at[g, j], rs_r.at[g, j])
            for zz in range(Z):
                value = pair_sum(g, j, zz)
                top = top_of(value, (0,))
                xy_q[g, j, zz] = coded(value, top)
                xy_c[g, j, pl.ds(zz, 1)] = top * (1.0 / LEVELS)
            send(xy_q.at[g, j], xy_r.at[g, j], rq_s.at[g, j], rq_r.at[g, j], peer)
            send(xy_c.at[g, j], xy_f.at[g, j], rc_s.at[g, j], rc_r.at[g, j], peer)

    def scatter_z(g):
        j = len(xy_peers)
        arrived(sib_in.at[g, group_at(j)], rs_s.at[g, j], rs_r.at[g, j])
        for i in range(j):
            arrived(xy_r.at[g, i], rq_s.at[g, i], rq_r.at[g, i])
            arrived(xy_f.at[g, i], rc_s.at[g, i], rc_r.at[g, i])

        def summed(zz):
            value = pair_sum(g, j, zz)
            for i in range(j):
                value = value + decoded(xy_r[g, i, zz], xy_f[g, i, pl.ds(zz, 1)])
            return value

        for d in range(1, Z):
            value = summed((z + d) % Z)
            top = top_of(value, (0,))
            z_q[g, d - 1] = coded(value, top)
            z_c[g, d - 1] = jnp.broadcast_to(top * (1.0 / LEVELS), (8, LANES))
            send(z_q.at[g, d - 1], z_r.at[g, d - 1], zq_s.at[g, d - 1], zq_r.at[g, d - 1], z_peers[d - 1])
            send(z_c.at[g, d - 1], z_f.at[g, d - 1], zc_s.at[g, d - 1], zc_r.at[g, d - 1], z_peers[d - 1])
        own[g] = summed(z)

    def scatter_end(g):
        value = own[g]
        for d in range(1, Z):
            arrived(z_r.at[g, d - 1], zq_s.at[g, d - 1], zq_r.at[g, d - 1])
            arrived(z_f.at[g, d - 1], zc_s.at[g, d - 1], zc_r.at[g, d - 1])
            value = value + decoded(z_r[g, d - 1], z_f[g, d - 1][:1])
        out[:, lanes(g)] = value

    for g in range(chunks):
        gather_z(g)
    load.wait()
    for g in range(chunks):
        gather_xy(g)
        if g == chunks - 1 and g:
            halo_recv(0)
        sources(g)
        halo_send(g)
    if chunks == 1:
        halo_recv(0)
    for g in range(chunks):
        halo_sides(g)
        sweeps(g)
        if g + 1 < chunks:
            halo_recv(g + 1)
        if g >= 2:
            scatter_z(g - 2)
        if g >= 1:
            scatter_xy(g - 1)
        forward(g)
    if chunks >= 2:
        scatter_z(chunks - 2)
    scatter_xy(chunks - 1)
    for g in range(chunks - 1):
        scatter_end(g)
    scatter_z(chunks - 1)
    scatter_end(chunks - 1)
    for has, copy in pending:
        if has is None:
            copy.wait_send()
        else:

            @pl.when(has)
            def _():
                copy.wait_send()


def local(operator_t, data_columns, noise_var, class_map, diffusion_table, kappa_table):
    rows, cols, data_rows = operator_t.shape
    count, width = data_columns.shape
    gx_size, gy_size = lax.axis_size("gx"), lax.axis_size("gy")
    X = 2
    Y, Z = gx_size // X, gy_size // 2
    chips = Y * X * Z
    points = rows * cols
    chunks = width // LANES
    m = ITERS
    start = count // 8 * 8
    H = max(up8(count), up8(2 * count) - start)
    tall = max(start + H, 2 * count)
    f32, bf16, i16, i32 = jnp.float32, jnp.bfloat16, jnp.int16, jnp.int32
    peers, zs = Y * X - 1, max(Z - 1, 1)

    def vmem(*shape, kind=f32):
        return pltpu.VMEM(shape, kind)

    def sems(*shape):
        return [pltpu.SemaphoreType.DMA(shape)] * 2

    field = (rows + 2 * m, cols + 2 * m)
    even = 2 * count % 8 == 0
    scratch = [
        vmem(points, data_rows, kind=bf16),
        vmem(chunks, Y, X, 2, Z, count, LANES, kind=bf16),
        vmem(data_rows, LANES),
        vmem(data_rows, LANES, kind=bf16),
        vmem(8, rows, LANES, kind=i32),
        vmem(4, *field, LANES),
        vmem(rows, cols, LANES),
        vmem(chunks, *field, LANES),
        vmem(*field, LANES),
        vmem(*field, LANES),
        vmem(chunks, rows, cols, LANES, kind=i16),
        vmem(chunks, 8, LANES),
        vmem(chunks, 2, m, cols, LANES, kind=i16),
        vmem(chunks, 2, 8, LANES),
        vmem(points, LANES, kind=bf16),
        vmem(*((8,) if even else (data_rows,)), LANES),
        vmem(chunks, Y * X, Z, tall, LANES),
        vmem(chunks, Y * X, Z, H, LANES),
        vmem(chunks, peers, Z, H, LANES, kind=i16),
        vmem(chunks, peers, Z, LANES),
        vmem(chunks, peers, Z, H, LANES, kind=i16),
        vmem(chunks, peers, Z, LANES),
        vmem(chunks, zs, H, LANES, kind=i16),
        vmem(chunks, zs, 8, LANES),
        vmem(chunks, zs, H, LANES, kind=i16),
        vmem(chunks, zs, 8, LANES),
        vmem(chunks, H, LANES),
        pltpu.SemaphoreType.DMA,
        *sems(8),
        *sems(chunks, zs),
        *sems(chunks, Z, peers),
        *sems(chunks, peers + 1),
        *sems(chunks, 2),
        *sems(chunks, 2),
        *sems(chunks, 2),
        *sems(chunks, 2, 2),
        *sems(chunks, peers + 1),
        *sems(chunks, peers),
        *sems(chunks, peers),
        *sems(chunks, zs),
        *sems(chunks, zs),
    ]
    block = pl.BlockSpec(memory_space=pltpu.VMEM)
    table = pl.BlockSpec(memory_space=pltpu.SMEM)
    classes = jnp.pad(class_map, ((0, 0), (0, LANES - cols)), constant_values=-1)
    out, prior = pl.pallas_call(
        functools.partial(block_kernel, (Y, X, Z), (gx_size, gy_size), start, H),
        out_shape=(
            jax.ShapeDtypeStruct((H, width), f32),
            jax.ShapeDtypeStruct((rows, cols, width), f32),
        ),
        in_specs=[block, block, table, table, pl.BlockSpec(memory_space=pl.ANY)],
        out_specs=(block, block),
        scratch_shapes=scratch,
        compiler_params=pltpu.CompilerParams(
            collective_id=0, has_side_effects=True, vmem_limit_bytes=60 << 20
        ),
    )(data_columns, classes, diffusion_table, kappa_table, operator_t.reshape(points, data_rows))
    core = lax.axis_index("gy") % 2
    forward = jnp.where(core == 0, out[:count], out[count - start : 2 * count - start])
    return (forward + noise_var[:, None] * data_columns.astype(f32), prior)


def solution(mesh):
    placed = (P("gx", "gy", None), P(("gx", "gy"), None), P(("gx", "gy")), P("gx", "gy"), P(), P())
    return jax.shard_map(
        local,
        mesh=mesh,
        in_specs=placed,
        out_specs=(P(("gx", "gy"), None), P("gx", "gy", None)),
        check_vma=False,
    )
```

```python
import functools
import jax
import jax.numpy as jnp
from jax import lax
from jax.experimental import pallas as pl
from jax.experimental.pallas import tpu as pltpu
from jax.sharding import PartitionSpec as P

ITERS = 8
LANES = 128
LEVELS = 32767.0
MESH = pl.DeviceIdType.MESH


def up8(n):
    return -(-n // 8) * 8


def remote(src, dst, send, recv, device):
    return pltpu.make_async_remote_copy(
        src_ref=src, dst_ref=dst, send_sem=send, recv_sem=recv, device_id=device, device_id_type=MESH
    )


def top_of(value, axes):
    return jnp.maximum(jnp.max(jnp.abs(value), axis=axes, keepdims=True), 1e-30)


def coded(value, top):
    return jnp.round(value * (LEVELS / top)).astype(jnp.int32).astype(jnp.int16)


def decoded(codes, scale):
    return codes.astype(jnp.int32).astype(jnp.float32) * scale


def block_kernel(
    dims, counts, start_row, H,
    mine, class_map, diffusion_table, kappa_table, operator_hbm,
    out, prior,
    operator, classes, full, stage, data, near_classes, coef, inverse,
    s, u, v, q_out, q_scale, q_in, q_in_scale, smooth,
    flat, wide, sib_in, xy_q, xy_c, xy_r, xy_f, z_q, z_c, z_r, z_f, own,
    op_sem, own_sem, cls_s, cls_r, gz_s, gz_r, gx_s, gx_r, gs_s, gs_r,
    hq_s, hq_r, hc_s, hc_r, he_s, he_r, hk_s, hk_r,
    rs_s, rs_r, rq_s, rq_r, rc_s, rc_r, zq_s, zq_r, zc_s, zc_r,
):
    Y, X, Z = dims
    m = ITERS
    chunks = s.shape[0]
    rows, cols = prior.shape[0], prior.shape[1]
    count = mine.shape[0]
    pair = 2 * count
    chips = Y * X * Z
    count_x, count_y = counts
    gx, gy = lax.axis_index("gx"), lax.axis_index("gy")
    y, x, z, me = gx // X, gx % X, gy // 2, gy % 2
    offsets = [(dy, dx) for dy in range(Y) for dx in range(X)][1:]
    offsets.sort(key=lambda d: (d[0] != 0) + (d[1] != 0))

    def device(y=y, x=x, z=z, core=me):
        return (y * X + x, z * 2 + core)

    sib = device(core=1 - me)
    z_peers = [device(z=(z + d) % Z) for d in range(1, Z)]
    xy_peers = [device(y=(y + dy) % Y, x=(x + dx) % X) for dy, dx in offsets]
    def exists(dr, dc):
        has = None
        for d, at, n in ((dr, gx, count_x), (dc, gy, count_y)):
            if d:
                ok = at > 0 if d < 0 else at < n - 1
                has = ok if has is None else has & ok
        return has

    def lanes(g):
        return pl.ds(g * LANES, LANES)

    pending = []

    def send(src, dst, sends, recvs, peer):
        copy = remote(src, dst, sends, recvs, peer)
        copy.start()
        pending.append((None, copy))

    def send_if(has, src, dst, sends, recvs, peer):
        copy = remote(src, dst, sends, recvs, peer)

        @pl.when(has)
        def _():
            copy.start()

        pending.append((has, copy))

    def arrived(ref, sends, recvs):
        remote(ref, ref, sends, recvs, sib).wait_recv()

    load = pltpu.make_async_copy(operator_hbm, operator, op_sem)
    load.start()
    homes = [
        pltpu.make_async_copy(mine.at[:, lanes(g)], full.at[g, y, x, me, z], own_sem.at[g])
        for g in range(chunks)
    ]
    for copy in homes:
        copy.start()
    classes[...] = jnp.full(classes.shape, -1, jnp.int32)
    classes[1, :, pl.ds(0, cols)] = class_map[...]

    wide_rows, wide_cols = rows + 2 * m, cols + 2 * m
    for (dr, dc), where in (
        ((-1, 0), (pl.ds(0, m), pl.ds(0, wide_cols))),
        ((1, 0), (pl.ds(m + rows, m), pl.ds(0, wide_cols))),
        ((0, -1), (pl.ds(0, wide_rows), pl.ds(0, m))),
        ((0, 1), (pl.ds(0, wide_rows), pl.ds(m + cols, m))),
    ):

        @pl.when(jnp.logical_not(exists(dr, dc)))
        def _():
            for g in range(chunks):
                s[g, where[0], where[1]] = jnp.zeros(
                    (where[0].size, where[1].size, LANES), jnp.float32
                )

    ready = pltpu.get_barrier_semaphore()
    for peer in [sib, *z_peers, *xy_peers]:
        pl.semaphore_signal(ready, inc=1, device_id=peer, device_id_type=MESH)
    beyond = gy + 2 * me - 1
    has_beyond = (beyond >= 0) & (beyond < count_y)

    @pl.when(has_beyond)
    def _():
        pl.semaphore_signal(ready, inc=1, device_id=(gx, beyond), device_id_type=MESH)

    pl.semaphore_wait(
        ready, 1 + len(z_peers) + len(xy_peers) + jnp.where(has_beyond, 1, 0)
    )

    north, south, west, east = (-1, 0), (1, 0), (0, -1), (0, 1)

    def peer_of(d):
        return (gx + d[0], gy + d[1])

    def class_sides_send():
        for i, (d, slot) in enumerate(((west, 2), (east, 0))):
            send_if(
                exists(*d), classes.at[1], classes.at[slot], cls_s.at[i], cls_r.at[i], peer_of(d)
            )

    def class_sides():
        for i, (d, slot) in enumerate(((east, 2), (west, 0))):

            @pl.when(exists(*d))
            def _():
                arrived(classes.at[slot], cls_s.at[i], cls_r.at[i])

        for i, (d, slot) in enumerate(((north, 1), (south, 0))):
            send_if(
                exists(*d), classes, near_classes.at[slot], cls_s.at[2 + i], cls_r.at[2 + i],
                peer_of(d),
            )

    class_sides_send()
    for copy in homes:
        copy.wait()
    for g in range(chunks):
        home = full.at[g, y, x, me, z]
        for d in range(1, Z):
            send(home, home, gz_s.at[g, d - 1], gz_r.at[g, d - 1], z_peers[d - 1])
        for j, peer in enumerate(xy_peers):
            send(home, home, gx_s.at[g, 0, j], gx_r.at[g, 0, j], peer)

    def coefficients():
        for i, (d, slot) in enumerate(((south, 1), (north, 0))):

            @pl.when(exists(*d))
            def _():
                arrived(near_classes.at[slot], cls_s.at[2 + i], cls_r.at[2 + i])

            @pl.when(jnp.logical_not(exists(*d)))
            def _():
                near_classes[slot] = jnp.full(near_classes.shape[1:], -1, jnp.int32)

        reach = m + 1
        lane = lax.broadcasted_iota(jnp.int32, (rows, LANES), 1)
        window = []
        for dr in (-1, 0, 1):
            held_at = (near_classes.at[0], classes, near_classes.at[1])[dr + 1]
            left = pltpu.roll(held_at[0], LANES - (cols - reach), 1)
            centre = pltpu.roll(held_at[1], reach, 1)
            right = pltpu.roll(held_at[2], reach + cols, 1)
            line = jnp.where(lane < reach, left, jnp.where(lane < reach + cols, centre, right))
            window.append(jnp.where(lane < 2 * reach + cols, line, -1))
        window = jnp.concatenate(window, axis=0)
        tall = 3 * rows
        diffusion = jnp.zeros((tall, LANES), jnp.float32)
        reaction = jnp.zeros((tall, LANES), jnp.float32)
        for k in range(diffusion_table.shape[0]):
            hit = window == k
            diffusion = jnp.where(hit, diffusion_table[k], diffusion)
            reaction = jnp.where(hit, kappa_table[k], reaction)
        inside = window >= 0
        weights = [
            0.5 * (diffusion + pltpu.roll(diffusion, shift, axis))
            for shift, axis in ((1, 0), (tall - 1, 0), (1, 1), (LANES - 1, 1))
        ]
        divisor = jnp.where(
            inside, reaction + weights[0] + weights[1] + weights[2] + weights[3], 1.0
        )

        def upright(values):
            values = pltpu.roll(values, LANES - 1, 1)[rows - m : rows - m + wide_rows]
            padded = jnp.concatenate(
                [values, jnp.zeros((LANES - wide_rows, LANES), jnp.float32)], axis=0
            )
            return padded.T

        for i, w in enumerate(weights):
            turned = upright(jnp.where(inside, w / divisor, 0.0))
            for r in range(wide_rows):
                coef[i, r] = jnp.broadcast_to(turned[:wide_cols, r : r + 1], (wide_cols, LANES))
        turned = upright(1.0 / divisor)
        for r in range(rows):
            inverse[r] = jnp.broadcast_to(turned[m : m + cols, m + r : m + r + 1], (cols, LANES))


    def held(g, d, core=me):
        return full.at[g, y, x, core, (z - d) % Z]

    def to_sibling(g, j):
        dy, dx = ([(0, 0)] + offsets)[j]
        group = full.at[g, (y - dy) % Y, (x - dx) % X, me]
        send(group, group, gs_s.at[g, j], gs_r.at[g, j], sib)

    def gather_z(g):
        for d in range(1, Z):
            block = held(g, d)
            arrived(block, gz_s.at[g, d - 1], gz_r.at[g, d - 1])
            for j, peer in enumerate(xy_peers):
                send(block, block, gx_s.at[g, d, j], gx_r.at[g, d, j], peer)
        to_sibling(g, 0)

    def gather_xy(g):
        packed(g, 0, me)
        for j, (dy, dx) in enumerate(offsets):
            for d in range(Z):
                block = full.at[g, (y - dy) % Y, (x - dx) % X, me, (z - d) % Z]
                arrived(block, gx_s.at[g, d, j], gx_r.at[g, d, j])
            to_sibling(g, j + 1)
            packed(g, j + 1, me)

    def packed(g, j, core):
        dy, dx = ([(0, 0)] + offsets)[j]
        yy, xx = (y - dy) % Y, (x - dx) % X
        size = 2 * Z * count
        place = stage.at[pl.ds(pl.multiple_of((yy * X + xx) * size, 8), size)]
        for zz in range(Z):
            for c in (0, 1):

                @pl.when(core == c)
                def _():
                    place[pl.ds((2 * zz + c) * count, count), :] = full[g, yy, xx, c, zz].astype(
                        jnp.float32
                    )

    def sources(g):
        for j, (dy, dx) in enumerate([(0, 0)] + offsets):
            group = full.at[g, (y - dy) % Y, (x - dx) % X, 1 - me]
            arrived(group, gs_s.at[g, j], gs_r.at[g, j])
            packed(g, j, 1 - me)
        data[...] = stage[...].astype(jnp.bfloat16)
        source = jnp.dot(operator[...], data[...], preferred_element_type=jnp.float32)
        tile = source.reshape(rows, cols, LANES) * inverse[...]
        s[g, pl.ds(m, rows), pl.ds(m, cols)] = tile
        top = top_of(tile, (0, 1))
        q_out[g] = coded(tile, top)
        q_scale[g] = jnp.broadcast_to(top[0] * (1.0 / LEVELS), (8, LANES))

    def halo_send(g):
        for i, (d, at) in enumerate(((north, 0), (south, rows - m))):
            has = exists(*d)
            send_if(
                has, q_out.at[g, pl.ds(at, m)], q_in.at[g, i], hq_s.at[g, i], hq_r.at[g, i],
                peer_of(d),
            )
            send_if(
                has, q_scale.at[g], q_in_scale.at[g, i], hc_s.at[g, i], hc_r.at[g, i], peer_of(d)
            )
        inner = pl.ds(m, rows)
        for i, (d, src, dst) in enumerate(((west, m, m + cols), (east, cols, 0))):
            send_if(
                exists(*d), s.at[g, inner, pl.ds(src, m)], s.at[g, inner, pl.ds(dst, m)],
                he_s.at[g, i], he_r.at[g, i], peer_of(d),
            )

    def halo_recv(g):
        for i, (d, at) in enumerate(((south, m + rows), (north, 0))):

            @pl.when(exists(*d))
            def _():
                arrived(q_in.at[g, i], hq_s.at[g, i], hq_r.at[g, i])
                arrived(q_in_scale.at[g, i], hc_s.at[g, i], hc_r.at[g, i])
                s[g, pl.ds(at, m), pl.ds(m, cols)] = decoded(
                    q_in[g, i], q_in_scale[g, i][:1][None]
                )

        for i, (d, src, dst) in enumerate(((west, m, m + cols), (east, cols, 0))):
            for k, at in enumerate((0, m + rows)):
                send_if(
                    exists(*d), s.at[g, pl.ds(at, m), pl.ds(src, m)],
                    s.at[g, pl.ds(at, m), pl.ds(dst, m)],
                    hk_s.at[g, i, k], hk_r.at[g, i, k], peer_of(d),
                )

    def halo_sides(g):
        for i, (d, dst) in enumerate(((east, m + cols), (west, 0))):

            @pl.when(exists(*d))
            def _():
                block = s.at[g, pl.ds(m, rows), pl.ds(dst, m)]
                arrived(block, he_s.at[g, i], he_r.at[g, i])
                for k, at in enumerate((0, m + rows)):
                    block = s.at[g, pl.ds(at, m), pl.ds(dst, m)]
                    arrived(block, hk_s.at[g, i, k], hk_r.at[g, i, k])

    def sweeps(g, hooks):
        turns = [u, v]
        fixed = s.at[g]
        for step in range(1, m + 1):
            if step in hooks:
                hooks[step]()
            old = fixed if step == 1 else turns[step % 2]
            new = turns[(step + 1) % 2]
            last = step == m

            def swept(r):
                centre = old[r]
                value = fixed[r] + coef[0, r] * old[r - 1]
                value = value + coef[1, r] * old[r + 1]
                value = value + coef[2, r] * pltpu.roll(centre, 1, 0)
                value = value + coef[3, r] * pltpu.roll(centre, wide_cols - 1, 0)
                if last:
                    done = value[m : m + cols]
                    prior[r - m, :, lanes(g)] = done
                    at = pl.multiple_of((r - m) * cols, cols)
                    smooth[pl.ds(at, cols), lanes(g)] = done.astype(jnp.bfloat16)
                else:
                    new[r] = value

            @pl.loop(0, (wide_rows - 2 * step) // 2)
            def _(i):
                swept(step + 2 * i)
                swept(step + 2 * i + 1)

    mine_rows = pl.ds(pl.multiple_of(me * start_row, 8), H)
    other_rows = pl.ds(pl.multiple_of((1 - me) * start_row, 8), H)
    groups = [*offsets, (0, 0)]

    def group_at(j):
        dy, dx = groups[j]
        return ((y + dy) % Y) * X + (x + dx) % X

    def forward(first, end):
        partial = lax.dot_general(
            operator[...], smooth[:, first * LANES : end * LANES], (((0,), (0,)), ((), ())),
            preferred_element_type=jnp.float32,
        )
        for g in range(first, end):
            part = partial[:, (g - first) * LANES : (g - first + 1) * LANES]
            if pair % 8 == 0:
                wide[g] = part.reshape(Y * X, Z, pair, LANES)
            else:
                flat[...] = part
                for k in range(chips):
                    wide[g, k // Z, k % Z, pl.ds(0, pair)] = flat[pl.ds(k * pair, pair)]
                    rest = wide.shape[3] - pair
                    wide[g, k // Z, k % Z, pl.ds(pair, rest)] = jnp.zeros(
                        (rest, LANES), jnp.float32
                    )
            for j in range(len(groups)):
                k = group_at(j)
                send(
                    wide.at[g, k, :, other_rows], sib_in.at[g, k], rs_s.at[g, j], rs_r.at[g, j],
                    sib,
                )

    def pair_sum(g, j, zz):
        k = group_at(j)
        return wide[g, k, zz, mine_rows] + sib_in[g, k, zz]

    turn = [*range(1, Z), 0]

    def scatter_xy(g):
        for j, peer in enumerate(xy_peers):
            k = group_at(j)
            arrived(sib_in.at[g, k], rs_s.at[g, j], rs_r.at[g, j])
            for d in range(Z):
                value = pair_sum(g, j, (z + turn[d]) % Z)
                top = top_of(value, (0,))
                xy_q[g, j, d] = coded(value, top)
                xy_c[g, j, pl.ds(d, 1)] = top * (1.0 / LEVELS)
            send(xy_c.at[g, j], xy_f.at[g, j], rc_s.at[g, j], rc_r.at[g, j], peer)
        for d in range(Z):
            for j, peer in enumerate(xy_peers):
                send(
                    xy_q.at[g, j, d], xy_r.at[g, j, d], rq_s.at[g, j, d], rq_r.at[g, j, d], peer
                )

    def scatter_z(g):
        j = len(xy_peers)
        arrived(sib_in.at[g, group_at(j)], rs_s.at[g, j], rs_r.at[g, j])
        for i in range(j):
            arrived(xy_f.at[g, i], rc_s.at[g, i], rc_r.at[g, i])
        for d in range(Z):
            value = pair_sum(g, j, (z + turn[d]) % Z)
            for i in range(j):
                arrived(xy_r.at[g, i, d], rq_s.at[g, i, d], rq_r.at[g, i, d])
                value = value + decoded(xy_r[g, i, d], xy_f[g, i, pl.ds(d, 1)])
            if d == Z - 1:
                own[g] = value
                break
            top = top_of(value, (0,))
            z_q[g, d] = coded(value, top)
            z_c[g, d] = jnp.broadcast_to(top * (1.0 / LEVELS), (8, LANES))
            send(z_c.at[g, d], z_f.at[g, d], zc_s.at[g, d], zc_r.at[g, d], z_peers[d])
            send(z_q.at[g, d], z_r.at[g, d], zq_s.at[g, d], zq_r.at[g, d], z_peers[d])

    def scatter_end(g):
        value = own[g]
        for d in range(1, Z):
            arrived(z_r.at[g, d - 1], zq_s.at[g, d - 1], zq_r.at[g, d - 1])
            arrived(z_f.at[g, d - 1], zc_s.at[g, d - 1], zc_r.at[g, d - 1])
            value = value + decoded(z_r[g, d - 1], z_f[g, d - 1][:1])
        out[:, lanes(g)] = value

    class_sides()
    for g in range(chunks):
        gather_z(g)
        if g == 0:
            coefficients()
    load.wait()
    for g in range(chunks):
        gather_xy(g)
        if g == chunks - 1 and g:
            halo_recv(0)
        sources(g)
        halo_send(g)
    if chunks == 1:
        halo_recv(0)
    waiting = []
    for g in range(chunks):
        halo_sides(g)
        hooks = {}
        if g + 1 < chunks:
            hooks[m // 2 + 1] = functools.partial(halo_recv, g + 1)
        for step, k in zip((m // 2 - 1, m - 1), waiting):
            hooks[step] = functools.partial(scatter_xy, k)
        sweeps(g, hooks)
        sent, waiting = waiting, []
        for k in sent[:1]:
            scatter_z(k)
        if g % 2 or g == chunks - 1:
            first = g - g % 2
            forward(first, g + 1)
            waiting = [*range(first, g + 1)]
        for k in sent[1:]:
            scatter_z(k)
    for k in waiting:
        scatter_xy(k)
    for k in range(waiting[0]):
        scatter_end(k)
    for k in waiting:
        scatter_z(k)
    for k in waiting:
        scatter_end(k)
    for has, copy in pending:
        if has is None:
            copy.wait_send()
        else:

            @pl.when(has)
            def _():
                copy.wait_send()


def local(operator_t, data_columns, noise_var, class_map, diffusion_table, kappa_table):
    rows, cols, data_rows = operator_t.shape
    count, width = data_columns.shape
    gx_size, gy_size = lax.axis_size("gx"), lax.axis_size("gy")
    X = 2
    Y, Z = gx_size // X, gy_size // 2
    chips = Y * X * Z
    points = rows * cols
    chunks = width // LANES
    m = ITERS
    start = count // 8 * 8
    H = max(up8(count), up8(2 * count) - start)
    tall = max(start + H, 2 * count)
    f32, bf16, i16, i32 = jnp.float32, jnp.bfloat16, jnp.int16, jnp.int32
    peers, zs = Y * X - 1, max(Z - 1, 1)

    def vmem(*shape, kind=f32):
        return pltpu.VMEM(shape, kind)

    def sems(*shape):
        return [pltpu.SemaphoreType.DMA(shape)] * 2

    field = (rows + 2 * m, cols + 2 * m)
    even = 2 * count % 8 == 0
    scratch = [
        vmem(points, data_rows, kind=bf16),
        vmem(3, rows, LANES, kind=i32),
        vmem(chunks, Y, X, 2, Z, count, LANES, kind=bf16),
        vmem(data_rows, LANES),
        vmem(data_rows, LANES, kind=bf16),
        vmem(2, 3, rows, LANES, kind=i32),
        vmem(4, *field, LANES),
        vmem(rows, cols, LANES),
        vmem(chunks, *field, LANES),
        vmem(*field, LANES),
        vmem(*field, LANES),
        vmem(chunks, rows, cols, LANES, kind=i16),
        vmem(chunks, 8, LANES),
        vmem(chunks, 2, m, cols, LANES, kind=i16),
        vmem(chunks, 2, 8, LANES),
        vmem(points, width, kind=bf16),
        vmem(*((8,) if even else (data_rows,)), LANES),
        vmem(chunks, Y * X, Z, tall, LANES),
        vmem(chunks, Y * X, Z, H, LANES),
        vmem(chunks, peers, Z, H, LANES, kind=i16),
        vmem(chunks, peers, Z, LANES),
        vmem(chunks, peers, Z, H, LANES, kind=i16),
        vmem(chunks, peers, Z, LANES),
        vmem(chunks, zs, H, LANES, kind=i16),
        vmem(chunks, zs, 8, LANES),
        vmem(chunks, zs, H, LANES, kind=i16),
        vmem(chunks, zs, 8, LANES),
        vmem(chunks, H, LANES),
        pltpu.SemaphoreType.DMA,
        pltpu.SemaphoreType.DMA((chunks,)),
        *sems(4),
        *sems(chunks, zs),
        *sems(chunks, Z, peers),
        *sems(chunks, peers + 1),
        *sems(chunks, 2),
        *sems(chunks, 2),
        *sems(chunks, 2),
        *sems(chunks, 2, 2),
        *sems(chunks, peers + 1),
        *sems(chunks, peers, Z),
        *sems(chunks, peers),
        *sems(chunks, zs),
        *sems(chunks, zs),
    ]
    block = pl.BlockSpec(memory_space=pltpu.VMEM)
    table = pl.BlockSpec(memory_space=pltpu.SMEM)
    anywhere = pl.BlockSpec(memory_space=pl.ANY)
    out, prior = pl.pallas_call(
        functools.partial(block_kernel, (Y, X, Z), (gx_size, gy_size), start, H),
        out_shape=(
            jax.ShapeDtypeStruct((H, width), f32),
            jax.ShapeDtypeStruct((rows, cols, width), f32),
        ),
        in_specs=[anywhere, block, table, table, anywhere],
        out_specs=(block, block),
        scratch_shapes=scratch,
        compiler_params=pltpu.CompilerParams(
            collective_id=0, has_side_effects=True, vmem_limit_bytes=52 << 20
        ),
    )(data_columns, class_map, diffusion_table, kappa_table, operator_t.reshape(points, data_rows))
    core = lax.axis_index("gy") % 2
    forward = jnp.where(core == 0, out[:count], out[count - start : 2 * count - start])
    return (forward + noise_var[:, None] * data_columns.astype(f32), prior)


def solution(mesh):
    placed = (P("gx", "gy", None), P(("gx", "gy"), None), P(("gx", "gy")), P("gx", "gy"), P(), P())
    return jax.shard_map(
        local,
        mesh=mesh,
        in_specs=placed,
        out_specs=(P(("gx", "gy"), None), P("gx", "gy", None)),
        check_vma=False,
    )
```

```python
import functools
import jax
import jax.numpy as jnp
from jax import lax
from jax.experimental import pallas as pl
from jax.experimental.pallas import tpu as pltpu
from jax.sharding import PartitionSpec as P

ITERS = 8
LANES = 128
LEVELS = 32767.0
MESH = pl.DeviceIdType.MESH


def up8(n):
    return -(-n // 8) * 8


def remote(src, dst, send, recv, device):
    return pltpu.make_async_remote_copy(
        src_ref=src, dst_ref=dst, send_sem=send, recv_sem=recv, device_id=device, device_id_type=MESH
    )


def top_of(value, axes):
    return jnp.maximum(jnp.max(jnp.abs(value), axis=axes, keepdims=True), 1e-30)


def coded(value, top):
    return jnp.round(value * (LEVELS / top)).astype(jnp.int32).astype(jnp.int16)


def decoded(codes, scale):
    return codes.astype(jnp.int32).astype(jnp.float32) * scale


def block_kernel(
    dims, counts, start_row, H,
    mine, class_map, diffusion_hbm, kappa_hbm, operator_hbm,
    out_hbm, prior_hbm,
    out, prior, class_in, diffusion_table, kappa_table, operator, classes, thin, full, stage, data, near_classes, coef, inverse,
    s, u, v, q_out, q_scale, q_in, q_in_scale, smooth,
    flat, wide, sib_in, xy_q, xy_c, xy_r, xy_f, z_q, z_c, z_r, z_f, own,
    op_sem, in_sem, out_sem, own_sem, cls_s, cls_r, gz_s, gz_r, gx_s, gx_r, gs_s, gs_r,
    hq_s, hq_r, hc_s, hc_r, he_s, he_r, hk_s, hk_r,
    rs_s, rs_r, rq_s, rq_r, rc_s, rc_r, zq_s, zq_r, zc_s, zc_r,
):
    Y, X, Z = dims
    m = ITERS
    chunks = s.shape[0]
    rows, cols = prior.shape[1], prior.shape[2]
    count = mine.shape[0]
    pair = 2 * count
    chips = Y * X * Z
    count_x, count_y = counts
    gx, gy = lax.axis_index("gx"), lax.axis_index("gy")
    y, x, z, me = gx // X, gx % X, gy // 2, gy % 2
    offsets = [(dy, dx) for dy in range(Y) for dx in range(X)][1:]
    offsets.sort(key=lambda d: (d[0] != 0) + (d[1] != 0))

    def device(y=y, x=x, z=z, core=me):
        return (y * X + x, z * 2 + core)

    sib = device(core=1 - me)
    z_peers = [device(z=(z + d) % Z) for d in range(1, Z)]
    xy_peers = [device(y=(y + dy) % Y, x=(x + dx) % X) for dy, dx in offsets]
    def exists(dr, dc):
        has = None
        for d, at, n in ((dr, gx, count_x), (dc, gy, count_y)):
            if d:
                ok = at > 0 if d < 0 else at < n - 1
                has = ok if has is None else has & ok
        return has

    def lanes(g):
        return pl.ds(g * LANES, LANES)

    pending, results = [], []

    def send(src, dst, sends, recvs, peer):
        copy = remote(src, dst, sends, recvs, peer)
        copy.start()
        pending.append((None, copy))

    def send_if(has, src, dst, sends, recvs, peer):
        copy = remote(src, dst, sends, recvs, peer)

        @pl.when(has)
        def _():
            copy.start()

        pending.append((has, copy))

    def arrived(ref, sends, recvs):
        remote(ref, ref, sends, recvs, sib).wait_recv()

    load = pltpu.make_async_copy(operator_hbm, operator, op_sem)
    load.start()
    homes = [
        pltpu.make_async_copy(mine.at[:, lanes(g)], full.at[g, y, x, me, z], own_sem.at[g])
        for g in range(chunks)
    ]
    for copy in homes:
        copy.start()
    small = [
        pltpu.make_async_copy(class_map, class_in, in_sem.at[0]),
        pltpu.make_async_copy(diffusion_hbm, diffusion_table, in_sem.at[1]),
        pltpu.make_async_copy(kappa_hbm, kappa_table, in_sem.at[2]),
    ]
    for copy in small:
        copy.start()
    classes[...] = jnp.full(classes.shape, -1, jnp.int32)

    wide_rows, wide_cols = rows + 2 * m, cols + 2 * m
    for (dr, dc), where in (
        ((-1, 0), (pl.ds(0, m), pl.ds(0, wide_cols))),
        ((1, 0), (pl.ds(m + rows, m), pl.ds(0, wide_cols))),
        ((0, -1), (pl.ds(0, wide_rows), pl.ds(0, m))),
        ((0, 1), (pl.ds(0, wide_rows), pl.ds(m + cols, m))),
    ):

        @pl.when(jnp.logical_not(exists(dr, dc)))
        def _():
            for g in range(chunks):
                s[g, where[0], where[1]] = jnp.zeros(
                    (where[0].size, where[1].size, LANES), jnp.float32
                )

    for copy in small:
        copy.wait()
    classes[1, :, pl.ds(0, cols)] = class_in[...]
    ready = pltpu.get_barrier_semaphore()
    for peer in [sib, *z_peers, *xy_peers]:
        pl.semaphore_signal(ready, inc=1, device_id=peer, device_id_type=MESH)
    beyond = gy + 2 * me - 1
    has_beyond = (beyond >= 0) & (beyond < count_y)

    @pl.when(has_beyond)
    def _():
        pl.semaphore_signal(ready, inc=1, device_id=(gx, beyond), device_id_type=MESH)

    pl.semaphore_wait(
        ready, 1 + len(z_peers) + len(xy_peers) + jnp.where(has_beyond, 1, 0)
    )

    north, south, west, east = (-1, 0), (1, 0), (0, -1), (0, 1)

    def peer_of(d):
        return (gx + d[0], gy + d[1])

    def class_sides_send():
        for i, (d, slot) in enumerate(((west, 2), (east, 0))):
            send_if(
                exists(*d), classes.at[1], classes.at[slot], cls_s.at[i], cls_r.at[i], peer_of(d)
            )

    def class_sides():
        for i, (d, slot) in enumerate(((east, 2), (west, 0))):

            @pl.when(exists(*d))
            def _():
                arrived(classes.at[slot], cls_s.at[i], cls_r.at[i])

        for i, (d, slot) in enumerate(((north, 1), (south, 0))):
            send_if(
                exists(*d), classes, near_classes.at[slot], cls_s.at[2 + i], cls_r.at[2 + i],
                peer_of(d),
            )

    class_sides_send()
    for copy in homes:
        copy.wait()
    for g in range(chunks):
        home = full.at[g, y, x, me, z]
        for d in range(1, Z):
            send(home, home, gz_s.at[g, d - 1], gz_r.at[g, d - 1], z_peers[d - 1])
        for j, peer in enumerate(xy_peers):
            send(home, home, gx_s.at[g, 0, j], gx_r.at[g, 0, j], peer)

    def coefficients():
        for i, (d, slot) in enumerate(((south, 1), (north, 0))):

            @pl.when(exists(*d))
            def _():
                arrived(near_classes.at[slot], cls_s.at[2 + i], cls_r.at[2 + i])

            @pl.when(jnp.logical_not(exists(*d)))
            def _():
                near_classes[slot] = jnp.full(near_classes.shape[1:], -1, jnp.int32)

        reach = m + 1
        lane = lax.broadcasted_iota(jnp.int32, (rows, LANES), 1)
        window = []
        for dr in (-1, 0, 1):
            held_at = (near_classes.at[0], classes, near_classes.at[1])[dr + 1]
            left = pltpu.roll(held_at[0], LANES - (cols - reach), 1)
            centre = pltpu.roll(held_at[1], reach, 1)
            right = pltpu.roll(held_at[2], reach + cols, 1)
            line = jnp.where(lane < reach, left, jnp.where(lane < reach + cols, centre, right))
            window.append(jnp.where(lane < 2 * reach + cols, line, -1))
        window = jnp.concatenate(window, axis=0)
        tall = 3 * rows
        diffusion = jnp.zeros((tall, LANES), jnp.float32)
        reaction = jnp.zeros((tall, LANES), jnp.float32)
        for k in range(diffusion_table.shape[0]):
            hit = window == k
            diffusion = jnp.where(hit, diffusion_table[k], diffusion)
            reaction = jnp.where(hit, kappa_table[k], reaction)
        inside = window >= 0
        weights = [
            0.5 * (diffusion + pltpu.roll(diffusion, shift, axis))
            for shift, axis in ((1, 0), (tall - 1, 0), (1, 1), (LANES - 1, 1))
        ]
        divisor = jnp.where(
            inside, reaction + weights[0] + weights[1] + weights[2] + weights[3], 1.0
        )

        def upright(values):
            values = pltpu.roll(values, LANES - 1, 1)[rows - m : rows - m + wide_rows]
            padded = jnp.concatenate(
                [values, jnp.zeros((LANES - wide_rows, LANES), jnp.float32)], axis=0
            )
            return padded.T

        for i, w in enumerate(weights):
            thin[i] = upright(jnp.where(inside, w / divisor, 0.0))
        turned = upright(1.0 / divisor)
        for r in range(rows):
            inverse[r] = jnp.broadcast_to(turned[m : m + cols, m + r : m + r + 1], (cols, LANES))


    def coefficient(i):
        turned = thin[i]
        for r in range(wide_rows):
            coef[i, r] = jnp.broadcast_to(turned[:wide_cols, r : r + 1], (wide_cols, LANES))

    def held(g, d, core=me):
        return full.at[g, y, x, core, (z - d) % Z]

    def to_sibling(g, j):
        dy, dx = ([(0, 0)] + offsets)[j]
        group = full.at[g, (y - dy) % Y, (x - dx) % X, me]
        send(group, group, gs_s.at[g, j], gs_r.at[g, j], sib)

    def gather_z(g):
        for d in range(1, Z):
            block = held(g, d)
            arrived(block, gz_s.at[g, d - 1], gz_r.at[g, d - 1])
            for j, peer in enumerate(xy_peers):
                send(block, block, gx_s.at[g, d, j], gx_r.at[g, d, j], peer)
        to_sibling(g, 0)

    def gather_xy(g):
        packed(g, 0, me)
        for j, (dy, dx) in enumerate(offsets):
            for d in range(Z):
                block = full.at[g, (y - dy) % Y, (x - dx) % X, me, (z - d) % Z]
                arrived(block, gx_s.at[g, d, j], gx_r.at[g, d, j])
            to_sibling(g, j + 1)
            packed(g, j + 1, me)

    def packed(g, j, core):
        dy, dx = ([(0, 0)] + offsets)[j]
        yy, xx = (y - dy) % Y, (x - dx) % X
        size = 2 * Z * count
        place = stage.at[pl.ds(pl.multiple_of((yy * X + xx) * size, 8), size)]
        for zz in range(Z):
            for c in (0, 1):

                @pl.when(core == c)
                def _():
                    place[pl.ds((2 * zz + c) * count, count), :] = full[g, yy, xx, c, zz].astype(
                        jnp.float32
                    )

    def sib_blocks(g):
        for j, (dy, dx) in enumerate([(0, 0)] + offsets):
            group = full.at[g, (y - dy) % Y, (x - dx) % X, 1 - me]
            arrived(group, gs_s.at[g, j], gs_r.at[g, j])
            packed(g, j, 1 - me)
        data[:, lanes(g)] = stage[...].astype(jnp.bfloat16)

    def sources(first, end):
        half = operator.shape[0] // 2
        right = data[:, first * LANES : end * LANES]
        source = jnp.concatenate(
            [
                jnp.dot(operator[rows_of, :], right, preferred_element_type=jnp.float32)
                for rows_of in (pl.ds(0, half), pl.ds(half, half))
            ],
            axis=0,
        )
        for g in range(first, end):
            part = source[:, (g - first) * LANES : (g - first + 1) * LANES]
            tile = part.reshape(rows, cols, LANES) * inverse[...]
            s[g, pl.ds(m, rows), pl.ds(m, cols)] = tile
            top = top_of(tile, (0, 1))
            q_out[g] = coded(tile, top)
            q_scale[g] = jnp.broadcast_to(top[0] * (1.0 / LEVELS), (8, LANES))
            halo_send(g)

    def halo_send(g):
        for i, (d, at) in enumerate(((north, 0), (south, rows - m))):
            has = exists(*d)
            send_if(
                has, q_out.at[g, pl.ds(at, m)], q_in.at[g, i], hq_s.at[g, i], hq_r.at[g, i],
                peer_of(d),
            )
            send_if(
                has, q_scale.at[g], q_in_scale.at[g, i], hc_s.at[g, i], hc_r.at[g, i], peer_of(d)
            )
        inner = pl.ds(m, rows)
        for i, (d, src, dst) in enumerate(((west, m, m + cols), (east, cols, 0))):
            send_if(
                exists(*d), s.at[g, inner, pl.ds(src, m)], s.at[g, inner, pl.ds(dst, m)],
                he_s.at[g, i], he_r.at[g, i], peer_of(d),
            )

    def halo_recv(g):
        for i, (d, at) in enumerate(((south, m + rows), (north, 0))):

            @pl.when(exists(*d))
            def _():
                arrived(q_in.at[g, i], hq_s.at[g, i], hq_r.at[g, i])
                arrived(q_in_scale.at[g, i], hc_s.at[g, i], hc_r.at[g, i])
                s[g, pl.ds(at, m), pl.ds(m, cols)] = decoded(
                    q_in[g, i], q_in_scale[g, i][:1][None]
                )

        for i, (d, src, dst) in enumerate(((west, m, m + cols), (east, cols, 0))):
            for k, at in enumerate((0, m + rows)):
                send_if(
                    exists(*d), s.at[g, pl.ds(at, m), pl.ds(src, m)],
                    s.at[g, pl.ds(at, m), pl.ds(dst, m)],
                    hk_s.at[g, i, k], hk_r.at[g, i, k], peer_of(d),
                )

    def halo_sides(g):
        for i, (d, dst) in enumerate(((east, m + cols), (west, 0))):

            @pl.when(exists(*d))
            def _():
                block = s.at[g, pl.ds(m, rows), pl.ds(dst, m)]
                arrived(block, he_s.at[g, i], he_r.at[g, i])
                for k, at in enumerate((0, m + rows)):
                    block = s.at[g, pl.ds(at, m), pl.ds(dst, m)]
                    arrived(block, hk_s.at[g, i, k], hk_r.at[g, i, k])

    def sweeps(g, hooks):
        turns = [u, v]
        fixed = s.at[g]
        for step in range(1, m + 1):
            if step in hooks:
                hooks[step]()
            old = fixed if step == 1 else turns[step % 2]
            new = turns[(step + 1) % 2]
            last = step == m

            def swept(r):
                centre = old[r]
                value = fixed[r] + coef[0, r] * old[r - 1]
                value = value + coef[1, r] * old[r + 1]
                value = value + coef[2, r] * pltpu.roll(centre, 1, 0)
                value = value + coef[3, r] * pltpu.roll(centre, wide_cols - 1, 0)
                if last:
                    done = value[m : m + cols]
                    prior[g, r - m] = done
                    at = pl.multiple_of((r - m) * cols, cols)
                    smooth[pl.ds(at, cols), lanes(g)] = done.astype(jnp.bfloat16)
                else:
                    new[r] = value

            @pl.loop(0, (wide_rows - 2 * step) // 2)
            def _(i):
                swept(step + 2 * i)
                swept(step + 2 * i + 1)

        results.append(
            pltpu.make_async_copy(prior.at[g], prior_hbm.at[:, :, lanes(g)], out_sem.at[1, g])
        )
        results[-1].start()

    mine_rows = pl.ds(pl.multiple_of(me * start_row, 8), H)
    other_rows = pl.ds(pl.multiple_of((1 - me) * start_row, 8), H)
    groups = [*offsets, (0, 0)]

    def group_at(j):
        dy, dx = groups[j]
        return ((y + dy) % Y) * X + (x + dx) % X

    def forward(first, end):
        total_rows = operator.shape[1]
        cut = -(-total_rows // 2 // LANES) * LANES
        right = smooth[:, first * LANES : end * LANES]
        partial = jnp.concatenate(
            [
                lax.dot_general(
                    operator[:, part], right, (((0,), (0,)), ((), ())),
                    preferred_element_type=jnp.float32,
                )
                for part in (pl.ds(0, cut), pl.ds(cut, total_rows - cut))
            ],
            axis=0,
        )
        for g in range(first, end):
            part = partial[:, (g - first) * LANES : (g - first + 1) * LANES]
            if pair % 8 == 0:
                wide[g] = part.reshape(Y * X, Z, pair, LANES)
            else:
                flat[...] = part
                for k in range(chips):
                    wide[g, k // Z, k % Z, pl.ds(0, pair)] = flat[pl.ds(k * pair, pair)]
                    rest = wide.shape[3] - pair
                    wide[g, k // Z, k % Z, pl.ds(pair, rest)] = jnp.zeros(
                        (rest, LANES), jnp.float32
                    )
            for j in range(len(groups)):
                k = group_at(j)
                send(
                    wide.at[g, k, :, other_rows], sib_in.at[g, k], rs_s.at[g, j], rs_r.at[g, j],
                    sib,
                )

    def pair_sum(g, j, zz):
        k = group_at(j)
        return wide[g, k, zz, mine_rows] + sib_in[g, k, zz]

    turn = [*range(1, Z), 0]

    def scatter_xy(g):
        for j, peer in enumerate(xy_peers):
            k = group_at(j)
            arrived(sib_in.at[g, k], rs_s.at[g, j], rs_r.at[g, j])
            for d in range(Z):
                value = pair_sum(g, j, (z + turn[d]) % Z)
                top = top_of(value, (0,))
                xy_q[g, j, d] = coded(value, top)
                xy_c[g, j, pl.ds(d, 1)] = top * (1.0 / LEVELS)
            send(xy_c.at[g, j], xy_f.at[g, j], rc_s.at[g, j], rc_r.at[g, j], peer)
        for d in range(Z):
            for j, peer in enumerate(xy_peers):
                send(
                    xy_q.at[g, j, d], xy_r.at[g, j, d], rq_s.at[g, j, d], rq_r.at[g, j, d], peer
                )

    def scatter_z(g):
        j = len(xy_peers)
        arrived(sib_in.at[g, group_at(j)], rs_s.at[g, j], rs_r.at[g, j])
        for i in range(j):
            arrived(xy_f.at[g, i], rc_s.at[g, i], rc_r.at[g, i])
        for d in range(Z):
            value = pair_sum(g, j, (z + turn[d]) % Z)
            for i in range(j):
                arrived(xy_r.at[g, i, d], rq_s.at[g, i, d], rq_r.at[g, i, d])
                value = value + decoded(xy_r[g, i, d], xy_f[g, i, pl.ds(d, 1)])
            if d == Z - 1:
                own[g] = value
                break
            top = top_of(value, (0,))
            z_q[g, d] = coded(value, top)
            z_c[g, d] = jnp.broadcast_to(top * (1.0 / LEVELS), (8, LANES))
            send(z_c.at[g, d], z_f.at[g, d], zc_s.at[g, d], zc_r.at[g, d], z_peers[d])
            send(z_q.at[g, d], z_r.at[g, d], zq_s.at[g, d], zq_r.at[g, d], z_peers[d])

    def scatter_end(g):
        value = own[g]
        for d in range(1, Z):
            arrived(z_r.at[g, d - 1], zq_s.at[g, d - 1], zq_r.at[g, d - 1])
            arrived(z_f.at[g, d - 1], zc_s.at[g, d - 1], zc_r.at[g, d - 1])
            value = value + decoded(z_r[g, d - 1], z_f[g, d - 1][:1])
        out[g] = value
        results.append(pltpu.make_async_copy(out.at[g], out_hbm.at[:, lanes(g)], out_sem.at[0, g]))
        results[-1].start()

    class_sides()
    for g in range(chunks):
        gather_z(g)
        if g == 0:
            coefficients()
        else:
            coefficient(g - 1)
    for i in range(chunks - 1, 4):
        coefficient(i)
    load.wait()
    gather_xy(0)
    sib_blocks(0)
    sources(0, 1)
    for g in range(1, chunks):
        gather_xy(g)
        sib_blocks(g)
        sources(g, g + 1)
    halo_recv(0)
    for g in range(chunks):
        halo_sides(g)
        sweeps(g, {2: functools.partial(scatter_xy, g - 1)} if g else {})
        if g + 1 < chunks:
            halo_recv(g + 1)
        forward(g, g + 1)
    last = chunks - 1
    for g in range(last - 1):
        scatter_z(g)
    scatter_xy(last)
    for g in range(max(last - 1, 0), last):
        scatter_z(g)
    for g in range(last):
        scatter_end(g)
    scatter_z(last)
    scatter_end(last)
    for copy in results:
        copy.wait()
    for has, copy in pending:
        if has is None:
            copy.wait_send()
        else:

            @pl.when(has)
            def _():
                copy.wait_send()


def local(operator_t, data_columns, noise_var, class_map, diffusion_table, kappa_table):
    rows, cols, data_rows = operator_t.shape
    count, width = data_columns.shape
    gx_size, gy_size = lax.axis_size("gx"), lax.axis_size("gy")
    X = 2
    Y, Z = gx_size // X, gy_size // 2
    chips = Y * X * Z
    points = rows * cols
    chunks = width // LANES
    m = ITERS
    start = count // 8 * 8
    H = max(up8(count), up8(2 * count) - start)
    tall = max(start + H, 2 * count)
    f32, bf16, i16, i32 = jnp.float32, jnp.bfloat16, jnp.int16, jnp.int32
    peers, zs = Y * X - 1, max(Z - 1, 1)

    def vmem(*shape, kind=f32):
        return pltpu.VMEM(shape, kind)

    def sems(*shape):
        return [pltpu.SemaphoreType.DMA(shape)] * 2

    field = (rows + 2 * m, cols + 2 * m)
    even = 2 * count % 8 == 0
    scratch = [
        vmem(chunks, H, LANES),
        vmem(chunks, rows, cols, LANES),
        vmem(rows, cols, kind=i32),
        pltpu.SMEM(diffusion_table.shape, f32),
        pltpu.SMEM(kappa_table.shape, f32),
        vmem(points, data_rows, kind=bf16),
        vmem(3, rows, LANES, kind=i32),
        vmem(4, LANES, LANES),
        vmem(chunks, Y, X, 2, Z, count, LANES, kind=bf16),
        vmem(data_rows, LANES),
        vmem(data_rows, width, kind=bf16),
        vmem(2, 3, rows, LANES, kind=i32),
        vmem(4, *field, LANES),
        vmem(rows, cols, LANES),
        vmem(chunks, *field, LANES),
        vmem(*field, LANES),
        vmem(*field, LANES),
        vmem(chunks, rows, cols, LANES, kind=i16),
        vmem(chunks, 8, LANES),
        vmem(chunks, 2, m, cols, LANES, kind=i16),
        vmem(chunks, 2, 8, LANES),
        vmem(points, width, kind=bf16),
        vmem(*((8,) if even else (data_rows,)), LANES),
        vmem(chunks, Y * X, Z, tall, LANES),
        vmem(chunks, Y * X, Z, H, LANES),
        vmem(chunks, peers, Z, H, LANES, kind=i16),
        vmem(chunks, peers, Z, LANES),
        vmem(chunks, peers, Z, H, LANES, kind=i16),
        vmem(chunks, peers, Z, LANES),
        vmem(chunks, zs, H, LANES, kind=i16),
        vmem(chunks, zs, 8, LANES),
        vmem(chunks, zs, H, LANES, kind=i16),
        vmem(chunks, zs, 8, LANES),
        vmem(chunks, H, LANES),
        pltpu.SemaphoreType.DMA,
        pltpu.SemaphoreType.DMA((3,)),
        pltpu.SemaphoreType.DMA((2, chunks)),
        pltpu.SemaphoreType.DMA((chunks,)),
        *sems(4),
        *sems(chunks, zs),
        *sems(chunks, Z, peers),
        *sems(chunks, peers + 1),
        *sems(chunks, 2),
        *sems(chunks, 2),
        *sems(chunks, 2),
        *sems(chunks, 2, 2),
        *sems(chunks, peers + 1),
        *sems(chunks, peers, Z),
        *sems(chunks, peers),
        *sems(chunks, zs),
        *sems(chunks, zs),
    ]
    anywhere = pl.BlockSpec(memory_space=pl.ANY)
    hbm = pl.BlockSpec(memory_space=pltpu.HBM)
    out, prior = pl.pallas_call(
        functools.partial(block_kernel, (Y, X, Z), (gx_size, gy_size), start, H),
        out_shape=(
            jax.ShapeDtypeStruct((H, width), f32),
            jax.ShapeDtypeStruct((rows, cols, width), f32),
        ),
        in_specs=[hbm] * 5,
        out_specs=(anywhere, anywhere),
        scratch_shapes=scratch,
        compiler_params=pltpu.CompilerParams(
            collective_id=0, has_side_effects=True, vmem_limit_bytes=52 << 20
        ),
    )(*[pltpu.with_memory_space_constraint(a, pltpu.HBM) for a in (data_columns, class_map, diffusion_table, kappa_table, operator_t.reshape(points, data_rows))])
    core = lax.axis_index("gy") % 2
    forward = jnp.where(core == 0, out[:count], out[count - start : 2 * count - start])
    return (forward + noise_var[:, None] * data_columns.astype(f32), prior)


def solution(mesh):
    placed = (P("gx", "gy", None), P(("gx", "gy"), None), P(("gx", "gy")), P("gx", "gy"), P(), P())
    return jax.shard_map(
        local,
        mesh=mesh,
        in_specs=placed,
        out_specs=(P(("gx", "gy"), None), P("gx", "gy", None)),
        check_vma=False,
    )
```

```python
import functools
import jax
import jax.numpy as jnp
from jax import lax
from jax.experimental import pallas as pl
from jax.experimental.pallas import tpu as pltpu
from jax.sharding import PartitionSpec as P

ITERS = 8
LANES = 128
LEVELS = 32767.0
MESH = pl.DeviceIdType.MESH


def up8(n):
    return -(-n // 8) * 8


def remote(src, dst, send, recv, device):
    return pltpu.make_async_remote_copy(
        src_ref=src, dst_ref=dst, send_sem=send, recv_sem=recv, device_id=device, device_id_type=MESH
    )


def top_of(value, axes):
    return jnp.maximum(jnp.max(jnp.abs(value), axis=axes, keepdims=True), 1e-30)


def coded(value, top):
    return jnp.round(value * (LEVELS / top)).astype(jnp.int32).astype(jnp.int16)


def decoded(codes, scale):
    return codes.astype(jnp.int32).astype(jnp.float32) * scale


def block_kernel(
    dims, counts, start_row, H,
    mine, class_map, diffusion_hbm, kappa_hbm, operator_hbm,
    out_hbm, prior_hbm,
    out, prior, class_in, diffusion_table, kappa_table, operator, classes, thin, full, stage, data, near_classes, coef, inverse,
    s, u, v, q_out, q_scale, q_in, q_in_scale, smooth,
    flat, wide, sib_in, xy_q, xy_c, xy_r, xy_f, z_q, z_c, z_r, z_f, own,
    op_sem, in_sem, out_sem, own_sem, cls_s, cls_r, gz_s, gz_r, gx_s, gx_r, gs_s, gs_r,
    hq_s, hq_r, hc_s, hc_r, he_s, he_r,
    rs_s, rs_r, rq_s, rq_r, rc_s, rc_r, zq_s, zq_r, zc_s, zc_r,
):
    Y, X, Z = dims
    m = ITERS
    chunks = s.shape[0]
    rows, cols = prior.shape[1], prior.shape[2]
    count = mine.shape[0]
    pair = 2 * count
    chips = Y * X * Z
    count_x, count_y = counts
    gx, gy = lax.axis_index("gx"), lax.axis_index("gy")
    y, x, z, me = gx // X, gx % X, gy // 2, gy % 2
    offsets = [(dy, dx) for dy in range(Y) for dx in range(X)][1:]
    offsets.sort(key=lambda d: (d[0] != 0) + (d[1] != 0))

    def device(y=y, x=x, z=z, core=me):
        return (y * X + x, z * 2 + core)

    sib = device(core=1 - me)
    z_peers = [device(z=(z + d) % Z) for d in range(1, Z)]
    xy_peers = [device(y=(y + dy) % Y, x=(x + dx) % X) for dy, dx in offsets]
    def exists(dr, dc):
        has = None
        for d, at, n in ((dr, gx, count_x), (dc, gy, count_y)):
            if d:
                ok = at > 0 if d < 0 else at < n - 1
                has = ok if has is None else has & ok
        return has

    def lanes(g):
        return pl.ds(g * LANES, LANES)

    pending = []

    def send(src, dst, sends, recvs, peer, has=None):
        if has is None:
            remote(src, dst, sends, recvs, peer).start()
        else:

            @pl.when(has)
            def _():
                remote(src, dst, sends, recvs, peer).start()

    def sent(ref, sends, has=None):
        pending.append((has, remote(ref, ref, sends, sends, sib)))

    def arrived(ref, recvs):
        remote(ref, ref, recvs, recvs, sib).wait_recv()

    load = pltpu.make_async_copy(operator_hbm, operator, op_sem)
    load.start()
    homes = [
        pltpu.make_async_copy(mine.at[:, lanes(g)], full.at[g, y, x, me, z], own_sem)
        for g in range(chunks)
    ]
    for copy in homes:
        copy.start()
    small = [
        pltpu.make_async_copy(class_map, class_in, in_sem.at[0]),
        pltpu.make_async_copy(diffusion_hbm, diffusion_table, in_sem.at[1]),
        pltpu.make_async_copy(kappa_hbm, kappa_table, in_sem.at[2]),
    ]
    for copy in small:
        copy.start()
    classes[...] = jnp.full(classes.shape, -1, jnp.int32)

    wide_rows, wide_cols = rows + 2 * m, cols + 2 * m
    for (dr, dc), where in (
        ((-1, 0), (pl.ds(0, m), pl.ds(0, wide_cols))),
        ((1, 0), (pl.ds(m + rows, m), pl.ds(0, wide_cols))),
        ((0, -1), (pl.ds(0, wide_rows), pl.ds(0, m))),
        ((0, 1), (pl.ds(0, wide_rows), pl.ds(m + cols, m))),
    ):

        @pl.when(jnp.logical_not(exists(dr, dc)))
        def _():
            for g in range(chunks):
                s[g, where[0], where[1]] = jnp.zeros(
                    (where[0].size, where[1].size, LANES), jnp.float32
                )

    for copy in small:
        copy.wait()
    classes[1, :, pl.ds(0, cols)] = class_in[...]
    ready = pltpu.get_barrier_semaphore()
    for peer in [sib, *z_peers, *xy_peers]:
        pl.semaphore_signal(ready, inc=1, device_id=peer, device_id_type=MESH)
    beyond = gy + 2 * me - 1
    has_beyond = (beyond >= 0) & (beyond < count_y)

    @pl.when(has_beyond)
    def _():
        pl.semaphore_signal(ready, inc=1, device_id=(gx, beyond), device_id_type=MESH)

    pl.semaphore_wait(
        ready, 1 + len(z_peers) + len(xy_peers) + jnp.where(has_beyond, 1, 0)
    )

    north, south, west, east = (-1, 0), (1, 0), (0, -1), (0, 1)

    def peer_of(d):
        return (gx + d[0], gy + d[1])

    def class_sides_send():
        for i, (d, slot) in enumerate(((west, 2), (east, 0))):
            has = exists(*d)
            send(classes.at[1], classes.at[slot], cls_s.at[i], cls_r.at[i], peer_of(d), has)
            sent(classes.at[1], cls_s.at[i], has)

    def class_sides():
        for i, (d, slot) in enumerate(((east, 2), (west, 0))):

            @pl.when(exists(*d))
            def _():
                arrived(classes.at[slot], cls_r.at[i])

        for i, (d, slot) in enumerate(((north, 1), (south, 0))):
            has, at = exists(*d), 2 + i
            send(classes, near_classes.at[slot], cls_s.at[at], cls_r.at[at], peer_of(d), has)
            sent(classes, cls_s.at[at], has)

    class_sides_send()
    home = full.at[:, y, x, me, z]
    pltpu.make_async_copy(home, home, own_sem).wait()
    for g in range(chunks):
        home = full.at[g, y, x, me, z]
        for d in range(1, Z):
            send(home, home, gz_s.at[g], gz_r.at[g, d - 1], z_peers[d - 1])
        for j, peer in enumerate(xy_peers):
            send(home, home, gx_s.at[g, j], gx_r.at[g, j], peer)
            sent(full.at[g, 0, 0, 0], gx_s.at[g, j])
        if Z > 1:
            sent(full.at[g, 0, 0, 0, pl.ds(0, Z - 1)], gz_s.at[g])
        sent(full.at[g, :, :, 0], gs_s.at[g])

    def coefficients():
        for i, (d, slot) in enumerate(((south, 1), (north, 0))):

            @pl.when(exists(*d))
            def _():
                arrived(near_classes.at[slot], cls_r.at[2 + i])

            @pl.when(jnp.logical_not(exists(*d)))
            def _():
                near_classes[slot] = jnp.full(near_classes.shape[1:], -1, jnp.int32)

        reach = m + 1
        lane = lax.broadcasted_iota(jnp.int32, (rows, LANES), 1)
        window = []
        for dr in (-1, 0, 1):
            held_at = (near_classes.at[0], classes, near_classes.at[1])[dr + 1]
            left = pltpu.roll(held_at[0], LANES - (cols - reach), 1)
            centre = pltpu.roll(held_at[1], reach, 1)
            right = pltpu.roll(held_at[2], reach + cols, 1)
            line = jnp.where(lane < reach, left, jnp.where(lane < reach + cols, centre, right))
            window.append(jnp.where(lane < 2 * reach + cols, line, -1))
        window = jnp.concatenate(window, axis=0)
        tall = 3 * rows
        diffusion = jnp.zeros((tall, LANES), jnp.float32)
        reaction = jnp.zeros((tall, LANES), jnp.float32)
        for k in range(diffusion_table.shape[0]):
            hit = window == k
            diffusion = jnp.where(hit, diffusion_table[k], diffusion)
            reaction = jnp.where(hit, kappa_table[k], reaction)
        inside = window >= 0
        weights = [
            0.5 * (diffusion + pltpu.roll(diffusion, shift, axis))
            for shift, axis in ((1, 0), (tall - 1, 0), (1, 1), (LANES - 1, 1))
        ]
        divisor = jnp.where(
            inside, reaction + weights[0] + weights[1] + weights[2] + weights[3], 1.0
        )

        def upright(values):
            values = pltpu.roll(values, LANES - 1, 1)[rows - m : rows - m + wide_rows]
            padded = jnp.concatenate(
                [values, jnp.zeros((LANES - wide_rows, LANES), jnp.float32)], axis=0
            )
            return padded.T

        for i, w in enumerate(weights):
            thin[i] = upright(jnp.where(inside, w / divisor, 0.0))
        turned = upright(1.0 / divisor)
        for r in range(rows):
            inverse[r] = jnp.broadcast_to(turned[m : m + cols, m + r : m + r + 1], (cols, LANES))


    def coefficient(i):
        turned = thin[i]
        for r in range(wide_rows):
            coef[i, r] = jnp.broadcast_to(turned[:wide_cols, r : r + 1], (wide_cols, LANES))

    def held(g, d, core=me):
        return full.at[g, y, x, core, (z - d) % Z]

    def to_sibling(g, j):
        dy, dx = ([(0, 0)] + offsets)[j]
        group = full.at[g, (y - dy) % Y, (x - dx) % X, me]
        send(group, group, gs_s.at[g], gs_r.at[g], sib)

    def gather_z(g):
        for d in range(1, Z):
            block = held(g, d)
            arrived(block, gz_r.at[g, d - 1])
            for j, peer in enumerate(xy_peers):
                send(block, block, gx_s.at[g, j], gx_r.at[g, j], peer)
        to_sibling(g, 0)

    def gather_xy(g):
        packed(g, 0, me)
        for j, (dy, dx) in enumerate(offsets):
            arrived(full.at[g, (y - dy) % Y, (x - dx) % X, me], gx_r.at[g, j])
            to_sibling(g, j + 1)
            packed(g, j + 1, me)

    def packed(g, j, core):
        dy, dx = ([(0, 0)] + offsets)[j]
        yy, xx = (y - dy) % Y, (x - dx) % X
        size = 2 * Z * count
        place = stage.at[pl.ds(pl.multiple_of((yy * X + xx) * size, 8), size)]
        for zz in range(Z):
            for c in (0, 1):

                @pl.when(core == c)
                def _():
                    place[pl.ds((2 * zz + c) * count, count), :] = full[g, yy, xx, c, zz].astype(
                        jnp.float32
                    )

    def sib_blocks(g):
        arrived(full.at[g, :, :, 1 - me], gs_r.at[g])
        for j in range(len(offsets) + 1):
            packed(g, j, 1 - me)
        data[:, lanes(g)] = stage[...].astype(jnp.bfloat16)

    def sources(first, end):
        half = operator.shape[0] // 2
        right = data[:, first * LANES : end * LANES]
        source = jnp.concatenate(
            [
                jnp.dot(operator[rows_of, :], right, preferred_element_type=jnp.float32)
                for rows_of in (pl.ds(0, half), pl.ds(half, half))
            ],
            axis=0,
        )
        for g in range(first, end):
            part = source[:, (g - first) * LANES : (g - first + 1) * LANES]
            tile = part.reshape(rows, cols, LANES) * inverse[...]
            s[g, pl.ds(m, rows), pl.ds(m, cols)] = tile
            top = top_of(tile, (0, 1))
            q_out[g] = coded(tile, top)
            q_scale[g] = top[0] * (1.0 / LEVELS)
            halo_send(g)

    strip = pl.ds(0, wide_rows)

    def halo_send(g):
        for i, (d, at) in enumerate(((north, 0), (south, rows - m))):
            has, peer = exists(*d), peer_of(d)
            send(q_out.at[g, pl.ds(at, m)], q_in.at[g, i], hq_s.at[g, i], hq_r.at[g, i], peer, has)
            send(q_scale.at[g], q_in_scale.at[g, i], hc_s.at[g, i], hc_r.at[g, i], peer, has)
            sent(q_in.at[g, i], hq_s.at[g, i], has)
            sent(q_scale.at[g], hc_s.at[g, i], has)
        inner = pl.ds(m, rows)
        for i, (d, src, dst) in enumerate(((west, m, m + cols), (east, cols, 0))):
            has = exists(*d)
            send(
                s.at[g, inner, pl.ds(src, m)], s.at[g, inner, pl.ds(dst, m)],
                he_s.at[g, i], he_r.at[g, i], peer_of(d), has,
            )
            sent(s.at[g, strip, pl.ds(src, m)], he_s.at[g, i], has)

    def halo_recv(g):
        for i, (d, at) in enumerate(((south, m + rows), (north, 0))):

            @pl.when(exists(*d))
            def _():
                arrived(q_in.at[g, i], hq_r.at[g, i])
                arrived(q_in_scale.at[g, i], hc_r.at[g, i])
                s[g, pl.ds(at, m), pl.ds(m, cols)] = decoded(q_in[g, i], q_in_scale[g, i][None])

        for i, (d, src, dst) in enumerate(((west, m, m + cols), (east, cols, 0))):
            for at in (0, m + rows):
                send(
                    s.at[g, pl.ds(at, m), pl.ds(src, m)], s.at[g, pl.ds(at, m), pl.ds(dst, m)],
                    he_s.at[g, i], he_r.at[g, i], peer_of(d), exists(*d),
                )

    def halo_sides(g):
        for i, (d, dst) in enumerate(((east, m + cols), (west, 0))):

            @pl.when(exists(*d))
            def _():
                arrived(s.at[g, strip, pl.ds(dst, m)], he_r.at[g, i])

    def sweeps(g, hooks):
        turns = [u, v]
        fixed = s.at[g]
        for step in range(1, m + 1):
            if step in hooks:
                hooks[step]()
            old = fixed if step == 1 else turns[step % 2]
            new = turns[(step + 1) % 2]
            last = step == m

            def swept(r):
                centre = old[r]
                value = fixed[r] + coef[0, r] * old[r - 1]
                value = value + coef[1, r] * old[r + 1]
                value = value + coef[2, r] * pltpu.roll(centre, 1, 0)
                value = value + coef[3, r] * pltpu.roll(centre, wide_cols - 1, 0)
                if last:
                    done = value[m : m + cols]
                    prior[g, r - m] = done
                    at = pl.multiple_of((r - m) * cols, cols)
                    smooth[pl.ds(at, cols), lanes(g)] = done.astype(jnp.bfloat16)
                else:
                    new[r] = value

            @pl.loop(0, (wide_rows - 2 * step) // 2)
            def _(i):
                swept(step + 2 * i)
                swept(step + 2 * i + 1)

        pltpu.make_async_copy(prior.at[g], prior_hbm.at[:, :, lanes(g)], out_sem.at[1]).start()

    mine_rows = pl.ds(pl.multiple_of(me * start_row, 8), H)
    other_rows = pl.ds(pl.multiple_of((1 - me) * start_row, 8), H)
    groups = [*offsets, (0, 0)]

    def group_at(j):
        dy, dx = groups[j]
        return ((y + dy) % Y) * X + (x + dx) % X

    turn = [*range(1, Z), 0]

    def forward(first, end):
        total_rows = operator.shape[1]
        cut = -(-total_rows // 2 // LANES) * LANES
        right = smooth[:, first * LANES : end * LANES]
        partial = jnp.concatenate(
            [
                lax.dot_general(
                    operator[:, part], right, (((0,), (0,)), ((), ())),
                    preferred_element_type=jnp.float32,
                )
                for part in (pl.ds(0, cut), pl.ds(cut, total_rows - cut))
            ],
            axis=0,
        )
        for g in range(first, end):
            part = partial[:, (g - first) * LANES : (g - first + 1) * LANES]
            if pair % 8 == 0:
                wide[g] = part.reshape(Y * X, Z, pair, LANES)
            else:
                flat[...] = part
                for k in range(chips):
                    wide[g, k // Z, k % Z, pl.ds(0, pair)] = flat[pl.ds(k * pair, pair)]
                    rest = wide.shape[3] - pair
                    wide[g, k // Z, k % Z, pl.ds(pair, rest)] = jnp.zeros(
                        (rest, LANES), jnp.float32
                    )
            for d in range(Z):
                zz = (z + turn[d]) % Z
                send(
                    wide.at[g, :, zz, other_rows], sib_in.at[g, :, zz], rs_s.at[g], rs_r.at[g, d],
                    sib,
                )
            sent(sib_in.at[g], rs_s.at[g])

    def pair_sum(g, j, zz):
        k = group_at(j)
        return wide[g, k, zz, mine_rows] + sib_in[g, k, zz]

    def scatter_xy(g):
        for d in range(Z):
            zz = (z + turn[d]) % Z
            arrived(sib_in.at[g, :, zz], rs_r.at[g, d])
            for j, peer in enumerate(xy_peers):
                value = pair_sum(g, j, zz)
                top = top_of(value, (0,))
                xy_q[g, d, j] = coded(value, top)
                xy_c[g, d, j] = top * (1.0 / LEVELS)
                send(xy_q.at[g, d, j], xy_r.at[g, d, j], rq_s.at[g], rq_r.at[g, d], peer)
                send(xy_c.at[g, d, j], xy_f.at[g, d, j], rc_s.at[g], rc_r.at[g, d], peer)
        sent(xy_q.at[g], rq_s.at[g])
        sent(xy_c.at[g], rc_s.at[g])

    def scatter_z(g):
        for d in range(Z):
            value = pair_sum(g, len(xy_peers), (z + turn[d]) % Z)
            arrived(xy_r.at[g, d], rq_r.at[g, d])
            arrived(xy_f.at[g, d], rc_r.at[g, d])
            for i in range(len(xy_peers)):
                value = value + decoded(xy_r[g, d, i], xy_f[g, d, i])
            if d == Z - 1:
                own[g] = value
                break
            top = top_of(value, (0,))
            z_q[g, d] = coded(value, top)
            z_c[g, d] = top * (1.0 / LEVELS)
            send(z_q.at[g, d], z_r.at[g, d], zq_s.at[g], zq_r.at[g], z_peers[d])
            send(z_c.at[g, d], z_f.at[g, d], zc_s.at[g], zc_r.at[g], z_peers[d])
        if Z > 1:
            sent(z_q.at[g], zq_s.at[g])
            sent(z_c.at[g], zc_s.at[g])

    def scatter_end(g):
        value = own[g]
        if Z > 1:
            arrived(z_r.at[g], zq_r.at[g])
            arrived(z_f.at[g], zc_r.at[g])
        for d in range(1, Z):
            value = value + decoded(z_r[g, d - 1], z_f[g, d - 1])
        out[g] = value
        pltpu.make_async_copy(out.at[g], out_hbm.at[:, lanes(g)], out_sem.at[0]).start()

    class_sides()
    for g in range(chunks):
        gather_z(g)
        if g == 0:
            coefficients()
        else:
            coefficient(g - 1)
    for i in range(chunks - 1, 4):
        coefficient(i)
    load.wait()
    gather_xy(0)
    sib_blocks(0)
    sources(0, 1)
    for g in range(1, chunks):
        gather_xy(g)
        sib_blocks(g)
        sources(g, g + 1)
    halo_recv(0)
    for g in range(chunks):
        halo_sides(g)
        sweeps(g, {m // 2 + 1: functools.partial(scatter_xy, g - 1)} if g else {})
        if g + 1 < chunks:
            halo_recv(g + 1)
        forward(g, g + 1)
    last = chunks - 1
    for g in range(last - 1):
        scatter_z(g)
    scatter_xy(last)
    for g in range(max(last - 1, 0), last):
        scatter_z(g)
    for g in range(last):
        scatter_end(g)
    scatter_z(last)
    scatter_end(last)
    pltpu.make_async_copy(prior_hbm, prior_hbm, out_sem.at[1]).wait()
    pltpu.make_async_copy(out_hbm, out_hbm, out_sem.at[0]).wait()
    for has, copy in pending:
        if has is None:
            copy.wait_send()
        else:

            @pl.when(has)
            def _():
                copy.wait_send()


def local(operator_t, data_columns, noise_var, class_map, diffusion_table, kappa_table):
    rows, cols, data_rows = operator_t.shape
    count, width = data_columns.shape
    gx_size, gy_size = lax.axis_size("gx"), lax.axis_size("gy")
    X = 2
    Y, Z = gx_size // X, gy_size // 2
    chips = Y * X * Z
    points = rows * cols
    chunks = width // LANES
    m = ITERS
    start = count // 8 * 8
    H = max(up8(count), up8(2 * count) - start)
    tall = max(start + H, 2 * count)
    f32, bf16, i16, i32 = jnp.float32, jnp.bfloat16, jnp.int16, jnp.int32
    peers, zs = Y * X - 1, max(Z - 1, 1)

    def vmem(*shape, kind=f32):
        return pltpu.VMEM(shape, kind)

    dma = pltpu.SemaphoreType.DMA

    def sems(*shapes):
        return [dma(shape) for shape in shapes]

    field = (rows + 2 * m, cols + 2 * m)
    even = 2 * count % 8 == 0
    scratch = [
        vmem(chunks, H, LANES),
        vmem(chunks, rows, cols, LANES),
        vmem(rows, cols, kind=i32),
        pltpu.SMEM(diffusion_table.shape, f32),
        pltpu.SMEM(kappa_table.shape, f32),
        vmem(points, data_rows, kind=bf16),
        vmem(3, rows, LANES, kind=i32),
        vmem(4, LANES, LANES),
        vmem(chunks, Y, X, 2, Z, count, LANES, kind=bf16),
        vmem(data_rows, LANES),
        vmem(data_rows, width, kind=bf16),
        vmem(2, 3, rows, LANES, kind=i32),
        vmem(4, *field, LANES),
        vmem(rows, cols, LANES),
        vmem(chunks, *field, LANES),
        vmem(*field, LANES),
        vmem(*field, LANES),
        vmem(chunks, rows, cols, LANES, kind=i16),
        vmem(chunks, 1, LANES),
        vmem(chunks, 2, m, cols, LANES, kind=i16),
        vmem(chunks, 2, 1, LANES),
        vmem(points, width, kind=bf16),
        vmem(*((8,) if even else (data_rows,)), LANES),
        vmem(chunks, Y * X, Z, tall, LANES),
        vmem(chunks, Y * X, Z, H, LANES),
        vmem(chunks, Z, peers, H, LANES, kind=i16),
        vmem(chunks, Z, peers, 1, LANES),
        vmem(chunks, Z, peers, H, LANES, kind=i16),
        vmem(chunks, Z, peers, 1, LANES),
        vmem(chunks, zs, H, LANES, kind=i16),
        vmem(chunks, zs, 1, LANES),
        vmem(chunks, zs, H, LANES, kind=i16),
        vmem(chunks, zs, 1, LANES),
        vmem(chunks, H, LANES),
        dma,
        dma((3,)),
        dma((2,)),
        dma,
        dma((4,)),
        dma((4,)),
        *sems((chunks,), (chunks, zs)),
        *sems((chunks, peers), (chunks, peers)),
        *sems((chunks,), (chunks,)),
        *sems((chunks, 2), (chunks, 2)),
        *sems((chunks, 2), (chunks, 2)),
        *sems((chunks, 2), (chunks, 2)),
        *sems((chunks,), (chunks, Z)),
        *sems((chunks,), (chunks, Z)),
        *sems((chunks,), (chunks, Z)),
        *sems((chunks,), (chunks,)),
        *sems((chunks,), (chunks,)),
    ]
    anywhere = pl.BlockSpec(memory_space=pl.ANY)
    hbm = pl.BlockSpec(memory_space=pltpu.HBM)
    out, prior = pl.pallas_call(
        functools.partial(block_kernel, (Y, X, Z), (gx_size, gy_size), start, H),
        out_shape=(
            jax.ShapeDtypeStruct((H, width), f32),
            jax.ShapeDtypeStruct((rows, cols, width), f32),
        ),
        in_specs=[hbm] * 5,
        out_specs=(anywhere, anywhere),
        scratch_shapes=scratch,
        compiler_params=pltpu.CompilerParams(
            collective_id=0, has_side_effects=True, vmem_limit_bytes=52 << 20
        ),
    )(*[pltpu.with_memory_space_constraint(a, pltpu.HBM) for a in (data_columns, class_map, diffusion_table, kappa_table, operator_t.reshape(points, data_rows))])
    core = lax.axis_index("gy") % 2
    forward = jnp.where(core == 0, out[:count], out[count - start : 2 * count - start])
    return (forward + noise_var[:, None] * data_columns.astype(f32), prior)


def solution(mesh):
    placed = (P("gx", "gy", None), P(("gx", "gy"), None), P(("gx", "gy")), P("gx", "gy"), P(), P())
    return jax.shard_map(
        local,
        mesh=mesh,
        in_specs=placed,
        out_specs=(P(("gx", "gy"), None), P("gx", "gy", None)),
        check_vma=False,
    )
```

```python
import functools
import jax
import jax.numpy as jnp
from jax import lax
from jax.experimental import pallas as pl
from jax.experimental.pallas import tpu as pltpu
from jax.sharding import PartitionSpec as P

ITERS = 8
LANES = 128
LEVELS = 32767.0
MESH = pl.DeviceIdType.MESH


def up8(n):
    return -(-n // 8) * 8


def remote(src, dst, send, recv, device):
    return pltpu.make_async_remote_copy(
        src_ref=src, dst_ref=dst, send_sem=send, recv_sem=recv, device_id=device, device_id_type=MESH
    )


def top_of(value, axes):
    return jnp.maximum(jnp.max(jnp.abs(value), axis=axes, keepdims=True), 1e-30)


def coded(value, top):
    return jnp.round(value * (LEVELS / top)).astype(jnp.int32).astype(jnp.int16)


def decoded(codes, scale):
    return codes.astype(jnp.int32).astype(jnp.float32) * scale


def block_kernel(
    dims, counts, start_row, H,
    mine, class_map, diffusion_hbm, kappa_hbm, operator_hbm,
    out_hbm, prior_hbm,
    out, prior, class_in, diffusion_table, kappa_table, operator, classes, thin, full, stage, data, near_classes, coef, inverse,
    s, fixed, u, v, line, q_out, q_scale, q_in, q_in_scale, smooth,
    flat, wide, sib_in, xy_q, xy_c, xy_r, xy_f, z_q, z_c, z_r, z_f, own,
    op_sem, in_sem, out_sem, own_sem, cls_s, cls_r, gz_s, gz_r, gx_s, gx_r, gs_s, gs_r,
    hq_s, hq_r, hc_s, hc_r, he_s, he_r,
    rs_s, rs_r, rq_s, rq_r, rc_s, rc_r, zq_s, zq_r, zc_s, zc_r,
):
    Y, X, Z = dims
    m = ITERS
    chunks = s.shape[0]
    rows, cols = prior.shape[1], prior.shape[2]
    count = mine.shape[0]
    pair = 2 * count
    chips = Y * X * Z
    count_x, count_y = counts
    gx, gy = lax.axis_index("gx"), lax.axis_index("gy")
    y, x, z, me = gx // X, gx % X, gy // 2, gy % 2
    offsets = [(dy, dx) for dy in range(Y) for dx in range(X)][1:]
    offsets.sort(key=lambda d: (d[0] != 0) + (d[1] != 0))

    def device(y=y, x=x, z=z, core=me):
        return (y * X + x, z * 2 + core)

    sib = device(core=1 - me)
    z_peers = [device(z=(z + d) % Z) for d in range(1, Z)]
    xy_peers = [device(y=(y + dy) % Y, x=(x + dx) % X) for dy, dx in offsets]
    def exists(dr, dc):
        has = None
        for d, at, n in ((dr, gx, count_x), (dc, gy, count_y)):
            if d:
                ok = at > 0 if d < 0 else at < n - 1
                has = ok if has is None else has & ok
        return has

    def lanes(g):
        return pl.ds(g * LANES, LANES)

    pending = []

    def send(src, dst, sends, recvs, peer, has=None):
        if has is None:
            remote(src, dst, sends, recvs, peer).start()
        else:

            @pl.when(has)
            def _():
                remote(src, dst, sends, recvs, peer).start()

    def sent(ref, sends, has=None):
        pending.append((has, remote(ref, ref, sends, sends, sib)))

    def arrived(ref, recvs):
        remote(ref, ref, recvs, recvs, sib).wait_recv()

    load = pltpu.make_async_copy(operator_hbm, operator, op_sem)
    load.start()
    homes = [
        pltpu.make_async_copy(mine.at[:, lanes(g)], full.at[g, y, x, me, z], own_sem)
        for g in range(chunks)
    ]
    for copy in homes:
        copy.start()
    small = [
        pltpu.make_async_copy(class_map, class_in, in_sem.at[0]),
        pltpu.make_async_copy(diffusion_hbm, diffusion_table, in_sem.at[1]),
        pltpu.make_async_copy(kappa_hbm, kappa_table, in_sem.at[2]),
    ]
    for copy in small:
        copy.start()
    classes[...] = jnp.full(classes.shape, -1, jnp.int32)

    wide_rows, wide_cols = rows + 2 * m, cols + 2 * m
    for (dr, dc), where in (
        ((-1, 0), (pl.ds(0, m), pl.ds(0, wide_cols))),
        ((1, 0), (pl.ds(m + rows, m), pl.ds(0, wide_cols))),
        ((0, -1), (pl.ds(0, wide_rows), pl.ds(0, m))),
        ((0, 1), (pl.ds(0, wide_rows), pl.ds(m + cols, m))),
    ):

        @pl.when(jnp.logical_not(exists(dr, dc)))
        def _():
            for g in range(chunks):
                s[g, where[0], where[1]] = jnp.zeros(
                    (where[0].size, where[1].size, LANES), jnp.float32
                )

    for copy in small:
        copy.wait()
    classes[1, :, pl.ds(0, cols)] = class_in[...]
    ready = pltpu.get_barrier_semaphore()
    for peer in [sib, *z_peers, *xy_peers]:
        pl.semaphore_signal(ready, inc=1, device_id=peer, device_id_type=MESH)
    beyond = gy + 2 * me - 1
    has_beyond = (beyond >= 0) & (beyond < count_y)

    @pl.when(has_beyond)
    def _():
        pl.semaphore_signal(ready, inc=1, device_id=(gx, beyond), device_id_type=MESH)

    pl.semaphore_wait(
        ready, 1 + len(z_peers) + len(xy_peers) + jnp.where(has_beyond, 1, 0)
    )

    north, south, west, east = (-1, 0), (1, 0), (0, -1), (0, 1)

    def peer_of(d):
        return (gx + d[0], gy + d[1])

    def class_sides_send():
        for i, (d, slot) in enumerate(((west, 2), (east, 0))):
            has = exists(*d)
            send(classes.at[1], classes.at[slot], cls_s.at[i], cls_r.at[i], peer_of(d), has)
            sent(classes.at[1], cls_s.at[i], has)

    def class_sides():
        for i, (d, slot) in enumerate(((east, 2), (west, 0))):

            @pl.when(exists(*d))
            def _():
                arrived(classes.at[slot], cls_r.at[i])

        for i, (d, slot) in enumerate(((north, 1), (south, 0))):
            has, at = exists(*d), 2 + i
            send(classes, near_classes.at[slot], cls_s.at[at], cls_r.at[at], peer_of(d), has)
            sent(classes, cls_s.at[at], has)

    class_sides_send()
    home = full.at[:, y, x, me, z]
    pltpu.make_async_copy(home, home, own_sem).wait()
    for g in range(chunks):
        home = full.at[g, y, x, me, z]
        for d in range(1, Z):
            send(home, home, gz_s.at[g], gz_r.at[g, d - 1], z_peers[d - 1])
        for j, peer in enumerate(xy_peers):
            send(home, home, gx_s.at[g, j], gx_r.at[g, j], peer)
            sent(full.at[g, 0, 0, 0], gx_s.at[g, j])
        if Z > 1:
            sent(full.at[g, 0, 0, 0, pl.ds(0, Z - 1)], gz_s.at[g])
        sent(full.at[g, :, :, 0], gs_s.at[g])

    def coefficients():
        for i, (d, slot) in enumerate(((south, 1), (north, 0))):

            @pl.when(exists(*d))
            def _():
                arrived(near_classes.at[slot], cls_r.at[2 + i])

            @pl.when(jnp.logical_not(exists(*d)))
            def _():
                near_classes[slot] = jnp.full(near_classes.shape[1:], -1, jnp.int32)

        reach = m + 1
        lane = lax.broadcasted_iota(jnp.int32, (rows, LANES), 1)
        window = []
        for dr in (-1, 0, 1):
            held_at = (near_classes.at[0], classes, near_classes.at[1])[dr + 1]
            left = pltpu.roll(held_at[0], LANES - (cols - reach), 1)
            centre = pltpu.roll(held_at[1], reach, 1)
            right = pltpu.roll(held_at[2], reach + cols, 1)
            line = jnp.where(lane < reach, left, jnp.where(lane < reach + cols, centre, right))
            window.append(jnp.where(lane < 2 * reach + cols, line, -1))
        window = jnp.concatenate(window, axis=0)
        tall = 3 * rows
        diffusion = jnp.zeros((tall, LANES), jnp.float32)
        reaction = jnp.zeros((tall, LANES), jnp.float32)
        for k in range(diffusion_table.shape[0]):
            hit = window == k
            diffusion = jnp.where(hit, diffusion_table[k], diffusion)
            reaction = jnp.where(hit, kappa_table[k], reaction)
        inside = window >= 0
        weights = [
            0.5 * (diffusion + pltpu.roll(diffusion, shift, axis))
            for shift, axis in ((1, 0), (tall - 1, 0), (1, 1), (LANES - 1, 1))
        ]
        divisor = jnp.where(
            inside, reaction + weights[0] + weights[1] + weights[2] + weights[3], 1.0
        )

        def upright(values):
            values = pltpu.roll(values, LANES - 1, 1)[rows - m : rows - m + wide_rows]
            padded = jnp.concatenate(
                [values, jnp.zeros((LANES - wide_rows, LANES), jnp.float32)], axis=0
            )
            return padded.T

        scale = 1.0 / jnp.sqrt(divisor)
        present = jnp.where(inside, scale, 0.0)
        for i, (w, shift, axis) in enumerate(
            ((weights[1], tall - 1, 0), (weights[3], LANES - 1, 1))
        ):
            thin[i] = upright(w * present * pltpu.roll(present, shift, axis))
        turned = upright(scale)
        for r in range(rows):
            inverse[r] = jnp.broadcast_to(turned[m : m + cols, m + r : m + r + 1], (cols, LANES))


    parts = wide_cols // 8

    def coefficient(i):
        for j in range(parts):
            turned = thin[i, pl.ds(j, 8, parts), :]
            for r in range(wide_rows):
                coef[i, r, j] = jnp.broadcast_to(turned[:, r : r + 1], (8, LANES))

    def held(g, d, core=me):
        return full.at[g, y, x, core, (z - d) % Z]

    def to_sibling(g, j):
        dy, dx = ([(0, 0)] + offsets)[j]
        group = full.at[g, (y - dy) % Y, (x - dx) % X, me]
        send(group, group, gs_s.at[g], gs_r.at[g], sib)

    def gather_z(g):
        for d in range(1, Z):
            block = held(g, d)
            arrived(block, gz_r.at[g, d - 1])
            for j, peer in enumerate(xy_peers):
                send(block, block, gx_s.at[g, j], gx_r.at[g, j], peer)
        to_sibling(g, 0)

    def gather_xy(g):
        packed(g, 0, me)
        for j, (dy, dx) in enumerate(offsets):
            arrived(full.at[g, (y - dy) % Y, (x - dx) % X, me], gx_r.at[g, j])
            to_sibling(g, j + 1)
            packed(g, j + 1, me)

    def packed(g, j, core):
        dy, dx = ([(0, 0)] + offsets)[j]
        yy, xx = (y - dy) % Y, (x - dx) % X
        size = 2 * Z * count
        place = stage.at[pl.ds(pl.multiple_of((yy * X + xx) * size, 8), size)]
        for zz in range(Z):
            for c in (0, 1):

                @pl.when(core == c)
                def _():
                    place[pl.ds((2 * zz + c) * count, count), :] = full[g, yy, xx, c, zz].astype(
                        jnp.float32
                    )

    def sib_blocks(g):
        arrived(full.at[g, :, :, 1 - me], gs_r.at[g])
        for j in range(len(offsets) + 1):
            packed(g, j, 1 - me)
        data[:, lanes(g)] = stage[...].astype(jnp.bfloat16)

    def sources(first, end):
        half = operator.shape[0] // 2
        right = data[:, first * LANES : end * LANES]
        source = jnp.concatenate(
            [
                jnp.dot(operator[rows_of, :], right, preferred_element_type=jnp.float32)
                for rows_of in (pl.ds(0, half), pl.ds(half, half))
            ],
            axis=0,
        )
        for g in range(first, end):
            part = source[:, (g - first) * LANES : (g - first + 1) * LANES]
            tile = part.reshape(rows, cols, LANES) * inverse[...]
            s[g, pl.ds(m, rows), pl.ds(m, cols)] = tile
            top = top_of(tile, (0, 1))
            q_out[g] = coded(tile, top)
            q_scale[g] = top[0] * (1.0 / LEVELS)
            halo_send(g)

    strip = pl.ds(0, wide_rows)

    def halo_send(g):
        for i, (d, at) in enumerate(((north, 0), (south, rows - m))):
            has, peer = exists(*d), peer_of(d)
            send(q_out.at[g, pl.ds(at, m)], q_in.at[g, i], hq_s.at[g, i], hq_r.at[g, i], peer, has)
            send(q_scale.at[g], q_in_scale.at[g, i], hc_s.at[g, i], hc_r.at[g, i], peer, has)
            sent(q_in.at[g, i], hq_s.at[g, i], has)
            sent(q_scale.at[g], hc_s.at[g, i], has)
        inner = pl.ds(m, rows)
        for i, (d, src, dst) in enumerate(((west, m, m + cols), (east, cols, 0))):
            has = exists(*d)
            send(
                s.at[g, inner, pl.ds(src, m)], s.at[g, inner, pl.ds(dst, m)],
                he_s.at[g, i], he_r.at[g, i], peer_of(d), has,
            )
            sent(s.at[g, strip, pl.ds(src, m)], he_s.at[g, i], has)

    def halo_recv(g):
        for i, (d, at) in enumerate(((south, m + rows), (north, 0))):

            @pl.when(exists(*d))
            def _():
                arrived(q_in.at[g, i], hq_r.at[g, i])
                arrived(q_in_scale.at[g, i], hc_r.at[g, i])
                s[g, pl.ds(at, m), pl.ds(m, cols)] = decoded(q_in[g, i], q_in_scale[g, i][None])

        for i, (d, src, dst) in enumerate(((west, m, m + cols), (east, cols, 0))):
            for at in (0, m + rows):
                send(
                    s.at[g, pl.ds(at, m), pl.ds(src, m)], s.at[g, pl.ds(at, m), pl.ds(dst, m)],
                    he_s.at[g, i], he_r.at[g, i], peer_of(d), exists(*d),
                )

    def halo_sides(g):
        for i, (d, dst) in enumerate(((east, m + cols), (west, 0))):

            @pl.when(exists(*d))
            def _():
                arrived(s.at[g, strip, pl.ds(dst, m)], he_r.at[g, i])

    def westward(row):
        return jnp.concatenate([pltpu.roll(row[parts - 1 :], 1, 1), row[: parts - 1]], axis=0)

    def eastward(row):
        return jnp.concatenate([row[1:], pltpu.roll(row[:1], 7, 1)], axis=0)

    def sweeps(g, hooks):
        turns = [u, v]

        @pl.loop(0, wide_rows)
        def _(r):
            for j in range(parts):
                fixed[r, j] = s[g, r, pl.ds(j, 8, parts)]

        for step in range(1, m + 1):
            if step in hooks:
                hooks[step]()
            old = fixed if step == 1 else turns[step % 2]
            new = turns[(step + 1) % 2]
            last = step == m

            def pair_of_rows(i, carry, step=step, old=old, new=new, last=last):
                flux, centre = carry
                for k in (0, 1):
                    r = step + 2 * i + k
                    down, right, below = coef[0, r], coef[1, r], old[r + 1]
                    value = fixed[r] + flux
                    value = value + down * below
                    value = value + westward(right * centre)
                    value = value + right * eastward(centre)
                    flux, centre = down * centre, below
                    if last:
                        for j in range(parts):
                            line[k, pl.ds(j, 8, parts)] = value[j]
                        done = line[k, pl.ds(m, cols)] * inverse[r - m]
                        prior[g, r - m] = done
                        at = pl.multiple_of((r - m) * cols, cols)
                        smooth[pl.ds(at, cols), lanes(g)] = done.astype(jnp.bfloat16)
                    else:
                        new[r] = value
                return flux, centre

            lax.fori_loop(
                0, (wide_rows - 2 * step) // 2, pair_of_rows,
                (coef[0, step - 1] * old[step - 1], old[step]),
            )

        pltpu.make_async_copy(prior.at[g], prior_hbm.at[:, :, lanes(g)], out_sem.at[1]).start()

    mine_rows = pl.ds(pl.multiple_of(me * start_row, 8), H)
    other_rows = pl.ds(pl.multiple_of((1 - me) * start_row, 8), H)
    groups = [*offsets, (0, 0)]

    def group_at(j):
        dy, dx = groups[j]
        return ((y + dy) % Y) * X + (x + dx) % X

    turn = [*range(1, Z), 0]

    def forward(first, end):
        total_rows = operator.shape[1]
        cut = -(-total_rows // 2 // LANES) * LANES
        left = smooth[:, first * LANES : end * LANES].T
        partial = jnp.concatenate(
            [
                jnp.dot(left, operator[:, part], preferred_element_type=jnp.float32).T
                for part in (pl.ds(0, cut), pl.ds(cut, total_rows - cut))
            ],
            axis=0,
        )
        for g in range(first, end):
            part = partial[:, (g - first) * LANES : (g - first + 1) * LANES]
            if pair % 8 == 0:
                wide[g] = part.reshape(Y * X, Z, pair, LANES)
            else:
                flat[...] = part
                for k in range(chips):
                    wide[g, k // Z, k % Z, pl.ds(0, pair)] = flat[pl.ds(k * pair, pair)]
                    rest = wide.shape[3] - pair
                    wide[g, k // Z, k % Z, pl.ds(pair, rest)] = jnp.zeros(
                        (rest, LANES), jnp.float32
                    )
            for d in range(Z):
                zz = (z + turn[d]) % Z
                send(
                    wide.at[g, :, zz, other_rows], sib_in.at[g, :, zz], rs_s.at[g], rs_r.at[g, d],
                    sib,
                )
            sent(sib_in.at[g], rs_s.at[g])

    def pair_sum(g, j, zz):
        k = group_at(j)
        return wide[g, k, zz, mine_rows] + sib_in[g, k, zz]

    def scatter_xy(g):
        for d in range(Z):
            zz = (z + turn[d]) % Z
            arrived(sib_in.at[g, :, zz], rs_r.at[g, d])
            for j, peer in enumerate(xy_peers):
                value = pair_sum(g, j, zz)
                top = top_of(value, (0,))
                xy_q[g, d, j] = coded(value, top)
                xy_c[g, d, j] = top * (1.0 / LEVELS)
                send(xy_q.at[g, d, j], xy_r.at[g, d, j], rq_s.at[g], rq_r.at[g, d], peer)
                send(xy_c.at[g, d, j], xy_f.at[g, d, j], rc_s.at[g], rc_r.at[g, d], peer)
        sent(xy_q.at[g], rq_s.at[g])
        sent(xy_c.at[g], rc_s.at[g])

    def scatter_z(g):
        for d in range(Z):
            value = pair_sum(g, len(xy_peers), (z + turn[d]) % Z)
            arrived(xy_r.at[g, d], rq_r.at[g, d])
            arrived(xy_f.at[g, d], rc_r.at[g, d])
            for i in range(len(xy_peers)):
                value = value + decoded(xy_r[g, d, i], xy_f[g, d, i])
            if d == Z - 1:
                own[g] = value
                break
            top = top_of(value, (0,))
            z_q[g, d] = coded(value, top)
            z_c[g, d] = top * (1.0 / LEVELS)
            send(z_q.at[g, d], z_r.at[g, d], zq_s.at[g], zq_r.at[g], z_peers[d])
            send(z_c.at[g, d], z_f.at[g, d], zc_s.at[g], zc_r.at[g], z_peers[d])
        if Z > 1:
            sent(z_q.at[g], zq_s.at[g])
            sent(z_c.at[g], zc_s.at[g])

    def scatter_end(g):
        value = own[g]
        if Z > 1:
            arrived(z_r.at[g], zq_r.at[g])
            arrived(z_f.at[g], zc_r.at[g])
        for d in range(1, Z):
            value = value + decoded(z_r[g, d - 1], z_f[g, d - 1])
        out[g] = value
        pltpu.make_async_copy(out.at[g], out_hbm.at[:, lanes(g)], out_sem.at[0]).start()

    class_sides()
    for g in range(chunks):
        gather_z(g)
        if g == 0:
            coefficients()
    load.wait()
    for g in range(chunks):
        gather_xy(g)
        if g in (1, 2):
            coefficient(g - 1)
        if g == chunks - 1 and g:
            halo_recv(0)
        sib_blocks(g)
        sources(g, g + 1)
    for i in range(chunks - 1, 2):
        coefficient(i)
    if chunks == 1:
        halo_recv(0)
    for g in range(chunks):
        halo_sides(g)
        hooks = {}
        if g:
            hooks[m // 2 + 1] = functools.partial(scatter_xy, g - 1)
        if g + 1 < chunks:
            hooks[m - 1] = functools.partial(halo_recv, g + 1)
        sweeps(g, hooks)
        forward(g, g + 1)
    last = chunks - 1
    for g in range(last - 1):
        scatter_z(g)
    scatter_xy(last)
    for g in range(max(last - 1, 0), chunks):
        scatter_z(g)
    for g in range(chunks):
        scatter_end(g)
    pltpu.make_async_copy(prior_hbm, prior_hbm, out_sem.at[1]).wait()
    pltpu.make_async_copy(out_hbm, out_hbm, out_sem.at[0]).wait()
    for has, copy in pending:
        if has is None:
            copy.wait_send()
        else:

            @pl.when(has)
            def _():
                copy.wait_send()


def local(operator_t, data_columns, noise_var, class_map, diffusion_table, kappa_table):
    rows, cols, data_rows = operator_t.shape
    count, width = data_columns.shape
    gx_size, gy_size = lax.axis_size("gx"), lax.axis_size("gy")
    X = 2
    Y, Z = gx_size // X, gy_size // 2
    chips = Y * X * Z
    points = rows * cols
    chunks = width // LANES
    m = ITERS
    start = count // 8 * 8
    H = max(up8(count), up8(2 * count) - start)
    tall = max(start + H, 2 * count)
    f32, bf16, i16, i32 = jnp.float32, jnp.bfloat16, jnp.int16, jnp.int32
    peers, zs = Y * X - 1, max(Z - 1, 1)

    def vmem(*shape, kind=f32):
        return pltpu.VMEM(shape, kind)

    dma = pltpu.SemaphoreType.DMA

    def sems(*shapes):
        return [dma(shape) for shape in shapes]

    field = (rows + 2 * m, cols + 2 * m)
    strided = (field[0], field[1] // 8, 8, LANES)
    even = 2 * count % 8 == 0
    scratch = [
        vmem(chunks, H, LANES),
        vmem(chunks, rows, cols, LANES),
        vmem(rows, cols, kind=i32),
        pltpu.SMEM(diffusion_table.shape, f32),
        pltpu.SMEM(kappa_table.shape, f32),
        vmem(points, data_rows, kind=bf16),
        vmem(3, rows, LANES, kind=i32),
        vmem(2, LANES, LANES),
        vmem(chunks, Y, X, 2, Z, count, LANES, kind=bf16),
        vmem(data_rows, LANES),
        vmem(data_rows, width, kind=bf16),
        vmem(2, 3, rows, LANES, kind=i32),
        vmem(2, *strided),
        vmem(rows, cols, LANES),
        vmem(chunks, *field, LANES),
        vmem(*strided),
        vmem(*strided),
        vmem(*strided),
        vmem(2, field[1], LANES),
        vmem(chunks, rows, cols, LANES, kind=i16),
        vmem(chunks, 1, LANES),
        vmem(chunks, 2, m, cols, LANES, kind=i16),
        vmem(chunks, 2, 1, LANES),
        vmem(points, width, kind=bf16),
        vmem(*((8,) if even else (data_rows,)), LANES),
        vmem(chunks, Y * X, Z, tall, LANES),
        vmem(chunks, Y * X, Z, H, LANES),
        vmem(chunks, Z, peers, H, LANES, kind=i16),
        vmem(chunks, Z, peers, 1, LANES),
        vmem(chunks, Z, peers, H, LANES, kind=i16),
        vmem(chunks, Z, peers, 1, LANES),
        vmem(chunks, zs, H, LANES, kind=i16),
        vmem(chunks, zs, 1, LANES),
        vmem(chunks, zs, H, LANES, kind=i16),
        vmem(chunks, zs, 1, LANES),
        vmem(chunks, H, LANES),
        dma,
        dma((3,)),
        dma((2,)),
        dma,
        dma((4,)),
        dma((4,)),
        *sems((chunks,), (chunks, zs)),
        *sems((chunks, peers), (chunks, peers)),
        *sems((chunks,), (chunks,)),
        *sems((chunks, 2), (chunks, 2)),
        *sems((chunks, 2), (chunks, 2)),
        *sems((chunks, 2), (chunks, 2)),
        *sems((chunks,), (chunks, Z)),
        *sems((chunks,), (chunks, Z)),
        *sems((chunks,), (chunks, Z)),
        *sems((chunks,), (chunks,)),
        *sems((chunks,), (chunks,)),
    ]
    anywhere = pl.BlockSpec(memory_space=pl.ANY)
    hbm = pl.BlockSpec(memory_space=pltpu.HBM)
    out, prior = pl.pallas_call(
        functools.partial(block_kernel, (Y, X, Z), (gx_size, gy_size), start, H),
        out_shape=(
            jax.ShapeDtypeStruct((H, width), f32),
            jax.ShapeDtypeStruct((rows, cols, width), f32),
        ),
        in_specs=[hbm] * 5,
        out_specs=(anywhere, anywhere),
        scratch_shapes=scratch,
        compiler_params=pltpu.CompilerParams(
            collective_id=0, has_side_effects=True, vmem_limit_bytes=52 << 20
        ),
    )(*[pltpu.with_memory_space_constraint(a, pltpu.HBM) for a in (data_columns, class_map, diffusion_table, kappa_table, operator_t.reshape(points, data_rows))])
    core = lax.axis_index("gy") % 2
    forward = jnp.where(core == 0, out[:count], out[count - start : 2 * count - start])
    return (forward + noise_var[:, None] * data_columns.astype(f32), prior)


def solution(mesh):
    placed = (P("gx", "gy", None), P(("gx", "gy"), None), P(("gx", "gy")), P("gx", "gy"), P(), P())
    return jax.shard_map(
        local,
        mesh=mesh,
        in_specs=placed,
        out_specs=(P(("gx", "gy"), None), P("gx", "gy", None)),
        check_vma=False,
    )
```
